32 devices in a mesh: fsdp: 32 (over z, y, x, core).
Axes of the slice: x: 2, y: 2, z: 4, core: 2. Of those that a mesh axis runs over, the one named last changes fastest.
Arguments:
- tokens: bfloat16 [4096, 1024], P('fsdp'), may hold values from -6 to 6
- cotangent: bfloat16 [4096, 1024], P('fsdp'), may hold values from -6 to 6
- lengths: int32 [32, 4], P('fsdp'), may hold values from 0 to 128, as said below
- offsets: int32 [32, 4], P('fsdp'), may hold values from 0 to 128, as said below
- norm_mix: bfloat16 [1024], P('fsdp'), may hold values from 0.5 to 1.5
- w_query: bfloat16 [1024, 512], P('fsdp'), may hold values from -0.1875 to 0.1875
- w_key: bfloat16 [1024, 512], P('fsdp'), may hold values from -0.1875 to 0.1875
- w_value: bfloat16 [1024, 1024], P('fsdp'), may hold values from -0.1875 to 0.1875
- w_gate: bfloat16 [1024, 1024], P('fsdp'), may hold values from -0.1875 to 0.1875
- w_betadecay: bfloat16 [1024, 8], P('fsdp'), may hold values from -0.1875 to 0.1875
- conv_weight: bfloat16 [2048, 4], P('fsdp'), may hold values from -3 to 3
- out_gain: bfloat16 [256], P('fsdp'), may hold values from 0.5 to 1.5
- w_out: bfloat16 [1024, 1024], P('fsdp'), may hold values from -0.1875 to 0.1875
- norm_ffn: bfloat16 [1024], P('fsdp'), may hold values from 0.5 to 1.5
- w_ffgate: bfloat16 [1024, 2816], P('fsdp'), may hold values from -0.1875 to 0.1875
- w_ffup: bfloat16 [1024, 2816], P('fsdp'), may hold values from -0.1875 to 0.1875
- w_ffdown: bfloat16 [2816, 1024], P('fsdp'), may hold values from -0.109375 to 0.109375
- decay_params: float32 [2, 4], replicated, may hold values from -6.5 to 1
Outputs:
- output: bfloat16 [4096, 1024], P('fsdp')
- input_grad: float32 [4096, 1024], P('fsdp')
- grad_norm_mix: float32 [1024], P('fsdp')
- grad_query: float32 [1024, 512], P('fsdp')
- grad_key: float32 [1024, 512], P('fsdp')
- grad_value: float32 [1024, 1024], P('fsdp')
- grad_gate: float32 [1024, 1024], P('fsdp')
- grad_betadecay: float32 [1024, 8], P('fsdp')
- grad_conv: float32 [2048, 4], P('fsdp')
- grad_out_gain: float32 [256], P('fsdp')
- grad_out: float32 [1024, 1024], P('fsdp')
- grad_norm_ffn: float32 [1024], P('fsdp')
- grad_ffgate: float32 [1024, 2816], P('fsdp')
- grad_ffup: float32 [1024, 2816], P('fsdp')
- grad_ffdown: float32 [2816, 1024], P('fsdp')
- grad_decay: float32 [2, 4], replicated
The draws below stay inside these ranges and needn't reach their ends.
Inputs may be any that keep to these rules, and one draw needn't show every extreme that they name: Row d lists the sequences packed in device d's 128 slots: entry s covers lengths[d, s] slots from slot offsets[d, s]. Used entries come first, in rising offset, without intersection, and each device has at least one; an unused entry has length 0 and offset 128. In every draw some device holds a single sequence of 128 slots. `offsets`: see lengths.
All inputs are finite; a program needn't handle non-finite values.
Results may differ from the reference program's by a relative error of at most 0.014.
The reference program's roundings to bfloat16 on the way count: a program that leaves them out, or rounds other values in their place, can miss the bound.
Values may be sent and summed in bfloat16 or wider, within the bound.
No kernel may reach another device: no remote copies, remote signals or barrier semaphores. Data moves between devices by JAX's collectives and lax.ppermute only.
A program may use at most 256 MiB of HBM per device.

```python
import jax
import jax.numpy as jnp
from jax import lax

D = 1024
H = 4
DK = 128
DV = 256
FF = 2816
CONV = 4
SLOTS = 128
SEQ_DEV = 4
KD = 512
VD = 1024
TOKENS = 4096
N_FSDP = 32


def packing(key):
    base_key = jax.random.fold_in(key, 11)
    key_count, key_jitter, key_gap, key_full = jax.random.split(base_key, 4)
    seq_count = jax.random.randint(key_count, (N_FSDP, 1), 1, SEQ_DEV + 1).astype(jnp.int32)
    base_span = (SLOTS // seq_count).astype(jnp.int32)
    reach = (base_span // (2 * seq_count)).astype(jnp.int32)
    raw_jitter = jax.random.randint(key_jitter, (N_FSDP, SEQ_DEV), 0, 1 << 20).astype(jnp.int32)
    jitter = (raw_jitter % (2 * reach + 1) - reach).astype(jnp.int32)
    entry_index = jnp.arange(SEQ_DEV, dtype=jnp.int32)[None, :]
    in_use = entry_index < seq_count
    before_last = entry_index < seq_count - 1
    spans = jnp.where(before_last, base_span + jitter, 0).astype(jnp.int32)
    head_total = jnp.sum(spans, axis=1, keepdims=True).astype(jnp.int32)
    spans = jnp.where(entry_index == seq_count - 1, SLOTS - head_total, spans).astype(jnp.int32)
    ends_sum = jnp.cumsum(spans, axis=1).astype(jnp.int32)
    starts = (ends_sum - spans).astype(jnp.int32)
    gap_sizes = jax.random.randint(key_gap, (N_FSDP, SEQ_DEV), 0, 3).astype(jnp.int32)
    gap_sizes = jnp.minimum(gap_sizes, spans - 1)
    seq_lengths = jnp.where(in_use, spans - gap_sizes, 0)
    seq_offsets = jnp.where(in_use, starts, SLOTS)
    full_row = jax.random.randint(key_full, (), 0, N_FSDP)
    row_index = jnp.arange(N_FSDP, dtype=jnp.int32)[:, None]
    single_len = jnp.where(entry_index == 0, SLOTS, 0)
    single_off = jnp.where(entry_index == 0, 0, SLOTS)
    seq_lengths = jnp.where(row_index == full_row, single_len, seq_lengths)
    seq_offsets = jnp.where(row_index == full_row, single_off, seq_offsets)
    return (seq_lengths.astype(jnp.int32), seq_offsets.astype(jnp.int32))


def draw_lengths(key, part):
    return packing(key)[0]


def draw_offsets(key, part):
    return packing(key)[1]


def draw_decay_params(key, part):
    key_rate, key_shift = jax.random.split(jax.random.fold_in(key, 5))
    log_rates = jax.random.uniform(key_rate, (1, H), jnp.float32, -6.0, -3.0)
    shifts = jax.random.uniform(key_shift, (1, H), jnp.float32, -1.0, 1.0)
    return jnp.concatenate([log_rates, shifts], axis=0)


def level_of(key, extent, cuts, low, top_value):
    level = 1.0
    for dim, parts in cuts:
        draws = jax.random.uniform(jax.random.fold_in(jax.random.fold_in(key, 6), dim), (parts,), jnp.float32, low / len(cuts), top_value / len(cuts))
        level = level * jnp.repeat(jnp.exp(draws), extent[dim] // parts).reshape((-1,) + (1,) * (len(extent) - 1 - dim))
    return level


def noise(own_key, shape, deviation, most, cuts=(), held_as=jnp.bfloat16):
    level = level_of(own_key, shape, cuts, -0.22, 0.18) if cuts else 1.0
    values = jax.random.normal(own_key, shape, jnp.float32) * deviation * level
    return jnp.minimum(jnp.maximum(values, -most), most).astype(held_as)


def setup_inputs(seed: int = 0) -> dict:
    seeds = jax.random.split(jax.random.key(seed), 19)
    tokens = noise(seeds[0], (TOKENS, D), 1.0, 6.0, ((0, 32),))
    cotangent = noise(seeds[1], (TOKENS, D), 1.0, 6.0, ((0, 32),))
    lengths = draw_lengths(jax.random.fold_in(seeds[18], 71), 0)
    offsets = draw_offsets(jax.random.fold_in(seeds[18], 71), 0)
    norm_mix = jnp.clip(1.0 + 0.1 * jax.random.normal(seeds[4], (D,), jnp.float32), 0.5, 1.5).astype(jnp.bfloat16)
    w_query = noise(seeds[5], (D, KD), D ** -0.5, 0.1875, ((0, 32),))
    w_key = noise(seeds[6], (D, KD), D ** -0.5, 0.1875, ((0, 32),))
    w_value = noise(seeds[7], (D, VD), D ** -0.5, 0.1875, ((0, 32),))
    w_gate = noise(seeds[8], (D, VD), D ** -0.5, 0.1875, ((0, 32),))
    w_betadecay = noise(seeds[9], (D, 2 * H), D ** -0.5, 0.1875, ((0, 32),))
    conv_weight = noise(seeds[10], (2 * KD + VD, CONV), CONV ** -0.5, 3.0, ((0, 32),))
    out_gain = jnp.clip(1.0 + 0.1 * jax.random.normal(seeds[11], (DV,), jnp.float32), 0.5, 1.5).astype(jnp.bfloat16)
    w_out = noise(seeds[12], (VD, D), VD ** -0.5, 0.1875, ((0, 32),))
    norm_ffn = jnp.clip(1.0 + 0.1 * jax.random.normal(seeds[13], (D,), jnp.float32), 0.5, 1.5).astype(jnp.bfloat16)
    w_ffgate = noise(seeds[14], (D, FF), D ** -0.5, 0.1875, ((0, 32),))
    w_ffup = noise(seeds[15], (D, FF), D ** -0.5, 0.1875, ((0, 32),))
    w_ffdown = noise(seeds[16], (FF, D), FF ** -0.5, 0.109375, ((0, 32),))
    decay_params = draw_decay_params(jax.random.fold_in(seeds[18], 71), 0)
    return {"tokens": tokens, "cotangent": cotangent, "lengths": lengths, "offsets": offsets, "norm_mix": norm_mix, "w_query": w_query, "w_key": w_key, "w_value": w_value, "w_gate": w_gate, "w_betadecay": w_betadecay, "conv_weight": conv_weight, "out_gain": out_gain, "w_out": w_out, "norm_ffn": norm_ffn, "w_ffgate": w_ffgate, "w_ffup": w_ffup, "w_ffdown": w_ffdown, "decay_params": decay_params}


highest_precision_mode = lax.Precision.HIGHEST

def matmul(left_side, right_side):
    return jnp.dot(left_side, right_side, preferred_element_type=jnp.float32)

def layout_masks(seq_lengths, seq_offsets, slots_count):
    slot_index = jnp.arange(slots_count, dtype=jnp.int32)
    inside = (slot_index[:, None] >= seq_offsets[None, :]) & (slot_index[:, None] < seq_offsets[None, :] + seq_lengths[None, :])
    is_valid = jnp.any(inside, axis=1)
    start_slot = lax.optimization_barrier(jnp.max(jnp.where(inside, seq_offsets[None, :], 0), axis=1)).astype(jnp.int32)
    start_slot = jnp.where(is_valid, start_slot, slot_index)
    return (start_slot, is_valid, start_slot == slot_index)

def rms_gain(values, gain_vec):
    return values * lax.rsqrt(lax.optimization_barrier(jnp.mean(values * values, axis=-1, keepdims=True)) + 1e-05) * gain_vec

def swiglu(gate_in, up_in):
    return jax.nn.silu(gate_in) * up_in

def short_conv(channels, conv_taps, start_slot):
    summed = channels * conv_taps[:, CONV - 1]
    for shift_by in range(1, CONV):
        shifted = jnp.concatenate([jnp.zeros((shift_by, channels.shape[1]), channels.dtype), channels[:-shift_by]], axis=0)
        earlier = jnp.concatenate([jnp.full((shift_by,), -1, jnp.int32), start_slot[:-shift_by]])
        same_seq = (earlier == start_slot)[:, None]
        summed = summed + jnp.where(same_seq, shifted, 0.0) * conv_taps[:, CONV - 1 - shift_by]
    return jax.nn.silu(summed)

def mixer_inputs(q_in, k_in, v_in, rate_in, conv_taps, decay_vec, start_slot):
    slots_count = q_in.shape[0]
    conv_out = short_conv(jnp.concatenate([q_in, k_in, v_in], axis=1), conv_taps, start_slot)
    queries = conv_out[:, :KD].reshape(slots_count, H, DK)
    keys = conv_out[:, KD:2 * KD].reshape(slots_count, H, DK)
    values = conv_out[:, 2 * KD:].reshape(slots_count, H, DV)
    queries = queries * lax.rsqrt(lax.optimization_barrier(jnp.sum(queries * queries, axis=-1, keepdims=True)) + 1e-06) * DK ** (-0.5)
    keys = keys * lax.rsqrt(lax.optimization_barrier(jnp.sum(keys * keys, axis=-1, keepdims=True)) + 1e-06)
    write_rate = jax.nn.sigmoid(rate_in[:, :H])
    logdecay = -jnp.exp(decay_vec[0]) * jax.nn.softplus(rate_in[:, H:] + decay_vec[1])
    return (queries, keys, values, write_rate, logdecay)

def finish_mixer(delta_out, gate_in, gain_vec):
    slots_count = delta_out.shape[0]
    normed = rms_gain(delta_out, gain_vec)
    gated = normed * jax.nn.silu(gate_in.reshape(slots_count, H, DV))
    return gated.reshape(slots_count, VD)

def delta_tokens(queries, keys, values, write_rate, logdecay, reset_slot):

    def advance(running_state_matrix, token_item):
        query_single_block, key_single_block, value_single_block, learning_rate_block, decay_one, reset_one = token_item
        factor = jnp.where(reset_one, 0.0, jnp.exp(decay_one))
        running_state_matrix = running_state_matrix * factor[:, None, None]
        predicted_values = jnp.einsum('oi,oif->of', key_single_block, running_state_matrix, precision=highest_precision_mode)
        running_state_matrix = running_state_matrix + jnp.einsum('ue,us->ues', key_single_block, learning_rate_block[:, None] * (value_single_block - predicted_values), precision=highest_precision_mode)
        return (running_state_matrix, jnp.einsum('oi,oif->of', query_single_block, running_state_matrix, precision=highest_precision_mode))
    init_state = jnp.zeros((queries.shape[1], queries.shape[2], values.shape[2]), jnp.float32)
    _, outputs = lax.scan(advance, init_state, (queries, keys, values, write_rate, logdecay, reset_slot))
    return outputs

def device_pass(tokens, cotangent, seq_lengths, seq_offsets, weights):
    norm_mix, w_query, w_key, w_value, w_gate, w_betadecay, conv_weight, out_gain, w_out, norm_ffn, w_ffgate, w_ffup, w_ffdown, decay_params = weights
    start_slot, is_valid, reset_slot = layout_masks(seq_lengths, seq_offsets, tokens.shape[0])
    tokens_wide = tokens.astype(jnp.float32)
    normed_in, back_norm_in = jax.vjp(rms_gain, tokens_wide, norm_mix.astype(jnp.float32))
    mix_input = normed_in.astype(jnp.bfloat16)
    q_pre = matmul(mix_input, w_query)
    k_pre = matmul(mix_input, w_key)
    v_pre = matmul(mix_input, w_value)
    gate_pre = matmul(mix_input, w_gate)
    bd_pre = matmul(mix_input, w_betadecay)

    def mix_piece(q_in, k_in, v_in, gate_in, rate_in, conv_taps, gain_vec, decay_vec):
        queries, keys, values, write_rate, logdecay = mixer_inputs(q_in, k_in, v_in, rate_in, conv_taps, decay_vec, start_slot)
        delta_out = delta_tokens(queries, keys, values, write_rate, logdecay, reset_slot)
        return finish_mixer(delta_out, gate_in, gain_vec)
    mixed_wide, back_mix = jax.vjp(mix_piece, q_pre, k_pre, v_pre, gate_pre, bd_pre, conv_weight.astype(jnp.float32), out_gain.astype(jnp.float32), decay_params)
    mixed = mixed_wide.astype(jnp.bfloat16)
    residual = tokens_wide + matmul(mixed, w_out)
    normed_ffn, back_norm_ffn = jax.vjp(rms_gain, residual, norm_ffn.astype(jnp.float32))
    ffn_input = normed_ffn.astype(jnp.bfloat16)
    up_gate = matmul(ffn_input, w_ffgate)
    up_lin = matmul(ffn_input, w_ffup)
    act_wide, back_act = jax.vjp(swiglu, up_gate, up_lin)
    act_narrow = act_wide.astype(jnp.bfloat16)
    final = residual + matmul(act_narrow, w_ffdown)
    valid_col = is_valid[:, None]
    output = jnp.where(valid_col, final, 0.0).astype(jnp.bfloat16)
    top_grad = jnp.where(valid_col, cotangent.astype(jnp.float32), 0.0)
    top_narrow = top_grad.astype(jnp.bfloat16)
    grad_ffdown = matmul(act_narrow.T, top_narrow)
    d_act = matmul(top_narrow, w_ffdown.T)
    d_ffgate_wide, d_ffup_wide = back_act(d_act)
    d_ffgate = d_ffgate_wide.astype(jnp.bfloat16)
    d_ffup = d_ffup_wide.astype(jnp.bfloat16)
    grad_ffgate = matmul(ffn_input.T, d_ffgate)
    grad_ffup = matmul(ffn_input.T, d_ffup)
    d_ffin = matmul(d_ffgate, w_ffgate.T) + matmul(d_ffup, w_ffup.T)
    d_res_norm, grad_norm_ffn = back_norm_ffn(d_ffin)
    d_residual = top_grad + d_res_norm
    d_res_narrow = d_residual.astype(jnp.bfloat16)
    grad_out = matmul(mixed.T, d_res_narrow)
    d_mixed = matmul(d_res_narrow, w_out.T)
    d_q_wide, d_k_wide, d_v_wide, d_gt_wide, d_bd_wide, grad_conv, grad_out_gain, grad_decay = back_mix(d_mixed)
    d_q = d_q_wide.astype(jnp.bfloat16)
    d_k = d_k_wide.astype(jnp.bfloat16)
    d_v = d_v_wide.astype(jnp.bfloat16)
    d_gt = d_gt_wide.astype(jnp.bfloat16)
    d_bd = d_bd_wide.astype(jnp.bfloat16)
    grad_query = matmul(mix_input.T, d_q)
    grad_key = matmul(mix_input.T, d_k)
    grad_value = matmul(mix_input.T, d_v)
    grad_gate = matmul(mix_input.T, d_gt)
    grad_betadecay = matmul(mix_input.T, d_bd)
    d_min = matmul(d_q, w_query.T) + matmul(d_k, w_key.T) + matmul(d_v, w_value.T) + matmul(d_gt, w_gate.T) + matmul(d_bd, w_betadecay.T)
    d_tok_norm, grad_norm_mix = back_norm_in(d_min)
    input_grad = d_residual + d_tok_norm
    grads = (grad_norm_mix, grad_query, grad_key, grad_value, grad_gate, grad_betadecay, grad_conv, grad_out_gain, grad_out, grad_norm_ffn, grad_ffgate, grad_ffup, grad_ffdown, grad_decay)
    return (output, input_grad, grads)

def reference(tokens, cotangent, lengths, offsets, norm_mix, w_query, w_key, w_value, w_gate, w_betadecay, conv_weight, out_gain, w_out, norm_ffn, w_ffgate, w_ffup, w_ffdown, decay_params):
    weights = (norm_mix, w_query, w_key, w_value, w_gate, w_betadecay, conv_weight, out_gain, w_out, norm_ffn, w_ffgate, w_ffup, w_ffdown, decay_params)
    token_blocks = tokens.reshape(N_FSDP, SLOTS, D)
    cot_blocks = cotangent.reshape(N_FSDP, SLOTS, D)

    def visit(totals, device_item):
        tok_one, cot_one, len_one, off_one = device_item
        out_one, din_one, grads = device_pass(tok_one, cot_one, len_one, off_one, weights)
        return (tuple((left_side + right_side for left_side, right_side in zip(totals, grads))), (out_one, din_one))
    init_totals = tuple((jnp.zeros(weight_single_block.shape, jnp.float32) for weight_single_block in weights))
    totals, (outputs, in_grads) = lax.scan(visit, init_totals, (token_blocks, cot_blocks, lengths, offsets))
    return (outputs.reshape(TOKENS, D), in_grads.reshape(TOKENS, D), totals[0], totals[1], totals[2], totals[3], totals[4], totals[5], totals[6], totals[7], totals[8], totals[9], totals[10], totals[11], totals[12], totals[13])
```

```python
import functools

import jax
import jax.numpy as jnp
from jax import lax
from jax.experimental import pallas as pl
from jax.experimental.pallas import tpu as pltpu
from jax.sharding import PartitionSpec as P

H = 4
DK = 128
DV = 256
CONV = 4
KD = H * DK
VD = H * DV
QKV = 2 * KD + VD
SMALL = 128
F32 = jnp.float32
BF16 = jnp.bfloat16


def dot32(a, b, ca, cb):
    return lax.dot_general(
        a, b, (((ca,), (cb,)), ((), ())), preferred_element_type=F32, precision=lax.Precision.HIGHEST
    )


def mm(a, b):
    return jnp.dot(a, b, preferred_element_type=F32)


def mm_t(a, b):
    return lax.dot_general(a, b, (((1,), (1,)), ((), ())), preferred_element_type=F32)


def t_mm(a, b):
    return lax.dot_general(a, b, (((0,), (0,)), ((), ())), preferred_element_type=F32)


def sigmoid(v):
    return 1.0 / (1.0 + jnp.exp(-v))


def find_start(slot, len_ref, off_ref):
    start = slot
    for s in range(len_ref.shape[1]):
        first = off_ref[0, s]
        inside = (slot >= first) & (slot < first + len_ref[0, s])
        start = jnp.where(inside, first, start)
    return start


def conv_sum(pre, taps, keeps):
    total = pre * taps[CONV - 1 : CONV]
    for s in range(1, CONV):
        total = total + jnp.where(keeps[s], pltpu.roll(pre, s, 0), 0.0) * taps[CONV - 1 - s : CONV - s]
    return total


def conv_grad(pre, d_sum, taps, keeps):
    n = pre.shape[0]
    d_pre = d_sum * taps[CONV - 1 : CONV]
    d_taps = [None] * CONV
    d_taps[CONV - 1] = jnp.sum(d_sum * pre, axis=0, keepdims=True)
    for s in range(1, CONV):
        masked = jnp.where(keeps[s], d_sum, 0.0)
        d_pre = d_pre + pltpu.roll(masked, n - s, 0) * taps[CONV - 1 - s : CONV - s]
        d_taps[CONV - 1 - s] = jnp.sum(masked * pltpu.roll(pre, s, 0), axis=0, keepdims=True)
    return d_pre, d_taps


class Block:
    def __init__(self, len_ref, off_ref, bd, rate_row, shift_row):
        n = bd.shape[0]
        row = lax.broadcasted_iota(jnp.int32, (n, n), 0)
        col = lax.broadcasted_iota(jnp.int32, (n, n), 1)
        slot_c = lax.broadcasted_iota(jnp.int32, (n, 1), 0)
        slot_r = lax.broadcasted_iota(jnp.int32, (1, n), 1)
        start_c = find_start(slot_c, len_ref, off_ref)
        start_r = find_start(slot_r, len_ref, off_ref)
        same = start_c == start_r
        self.row, self.col = row, col
        self.low = same & (row >= col)
        self.strict = same & (row > col)
        self.keeps = [None] + [slot_c - s >= start_c for s in range(1, CONV)]
        self.low_f = jnp.where(self.low, 1.0, 0.0)
        self.beta = sigmoid(bd)
        shifted = bd + shift_row
        self.shifted = shifted
        self.soft = jnp.maximum(shifted, 0.0) + jnp.log1p(jnp.exp(-jnp.abs(shifted)))
        self.rate = jnp.exp(rate_row)
        self.logdecay = -self.rate * self.soft
        self.cum = dot32(self.low_f, self.logdecay, 1, 0)
        self.cum_t = self.cum.T

    def decay(self, h):
        gap = self.cum[:, H + h : H + h + 1] - self.cum_t[H + h : H + h + 1, :]
        return jnp.where(self.low, jnp.exp(jnp.where(self.low, gap, 0.0)), 0.0)


def unit(v):
    r = lax.rsqrt(jnp.sum(v * v, axis=-1, keepdims=True) + 1e-06)
    return v * r, r


def head_cols(h):
    return (
        slice(h * DK, (h + 1) * DK),
        slice(KD + h * DK, KD + (h + 1) * DK),
        slice(2 * KD + h * DV, 2 * KD + (h + 1) * DV),
        slice(QKV + h * DV, QKV + (h + 1) * DV),
    )


def mixer_fwd_kernel(len_ref, off_ref, pre_ref, taps_ref, gain_ref, dec_ref, mixed_ref, inv_ref, upd_ref, out_ref):
    n = pre_ref.shape[0]
    bd = pre_ref[:, QKV + VD : QKV + VD + SMALL]
    blk = Block(len_ref, off_ref, bd, dec_ref[0:1], dec_ref[1:2])
    gain = gain_ref[...]
    lows, scores, rhs = [], [], []
    for h in range(H):
        cq, ck, cv, cg = head_cols(h)

        def conv_silu(cols):
            y = conv_sum(pre_ref[:, cols], taps_ref[:, cols], blk.keeps)
            return y * sigmoid(y)

        q = unit(conv_silu(cq))[0] * DK ** (-0.5)
        k = unit(conv_silu(ck))[0]
        v = conv_silu(cv)
        beta = blk.beta[:, h : h + 1]
        decay = blk.decay(h)
        lows.append(jnp.where(blk.strict, beta * decay * dot32(k, k, 1, 1), 0.0))
        scores.append(decay * dot32(q, k, 1, 1))
        rhs.append(beta * v)
    inv = []
    eye = jnp.where(blk.row == blk.col, 1.0, 0.0)
    pair = (blk.row // 2 == blk.col // 2) & (blk.row > blk.col)
    for h in range(H):
        inv.append(eye - jnp.where(pair, lows[h], 0.0))
    size = 2
    while size < n:
        part = (blk.row // (2 * size) == blk.col // (2 * size)) & (blk.row // size > blk.col // size)
        mids = [dot32(jnp.where(part, lows[h], 0.0), inv[h], 1, 0) for h in range(H)]
        inv = [inv[h] - dot32(inv[h], mids[h], 1, 0) for h in range(H)]
        size *= 2
    for h in range(H):
        _, _, _, cg = head_cols(h)
        cols = slice(h * DV, (h + 1) * DV)
        upd = dot32(inv[h], rhs[h], 1, 0)
        out = dot32(scores[h], upd, 1, 0)
        inv_ref[:, h * n : (h + 1) * n] = inv[h]
        upd_ref[:, cols] = upd
        out_ref[:, cols] = out
        r = lax.rsqrt(jnp.mean(out * out, axis=-1, keepdims=True) + 1e-05)
        gate = pre_ref[:, cg]
        mixed_ref[:, cols] = (out * r * gain * (gate * sigmoid(gate))).astype(BF16)


def mixer_bwd_kernel(
    len_ref, off_ref, pre_ref, taps_ref, gain_ref, dec_ref, inv_ref, upd_ref, out_ref, dmix_ref,
    dpre_ref, dtaps_ref, dgain_ref, ddec_ref,
):
    n = pre_ref.shape[0]
    bd = pre_ref[:, QKV + VD : QKV + VD + SMALL]
    blk = Block(len_ref, off_ref, bd, dec_ref[0:1], dec_ref[1:2])
    gain = gain_ref[...]
    lane = lax.broadcasted_iota(jnp.int32, (n, SMALL), 1)
    d_gain = jnp.zeros((1, DV), F32)
    d_beta = jnp.zeros((n, SMALL), F32)
    d_cum = jnp.zeros((n, SMALL), F32)
    for h in range(H):
        cq, ck, cv, cg = head_cols(h)
        cols = slice(h * DV, (h + 1) * DV)
        out = out_ref[:, cols]
        gate = pre_ref[:, cg]
        d_mixed = dmix_ref[:, cols]
        r = lax.rsqrt(jnp.mean(out * out, axis=-1, keepdims=True) + 1e-05)
        sg = sigmoid(gate)
        silu_g = gate * sg
        unit_out = out * r
        d_normed = d_mixed * silu_g
        dpre_ref[:, cg] = (d_mixed * unit_out * gain * (sg * (1.0 + gate * (1.0 - sg)))).astype(BF16)
        d_gain = d_gain + jnp.sum(d_normed * unit_out, axis=0, keepdims=True)
        d_hat = d_normed * gain
        d_out = r * d_hat - out * (r * r * r) * jnp.mean(d_hat * out, axis=-1, keepdims=True)

        def conv_silu(cols_in):
            y = conv_sum(pre_ref[:, cols_in], taps_ref[:, cols_in], blk.keeps)
            s = sigmoid(y)
            return y * s, s * (1.0 + y * (1.0 - s))

        q_raw, q_slope = conv_silu(cq)
        k_raw, k_slope = conv_silu(ck)
        v, v_slope = conv_silu(cv)
        q_unit, q_r = unit(q_raw)
        k, k_r = unit(k_raw)
        scale = DK ** (-0.5)
        q = q_unit * scale
        beta = blk.beta[:, h : h + 1]
        decay = blk.decay(h)
        kk = dot32(k, k, 1, 1)
        qk = dot32(q, k, 1, 1)
        inv = inv_ref[:, h * n : (h + 1) * n]
        upd = upd_ref[:, cols]
        d_score = dot32(d_out, upd, 1, 1)
        d_upd = dot32(decay * qk, d_out, 0, 0)
        d_rhs = dot32(inv, d_upd, 0, 0)
        d_low = jnp.where(blk.strict, -dot32(d_rhs, upd, 1, 1), 0.0)
        dl = d_low * decay
        d_kk = dl * beta
        d_qk = d_score * decay
        d_beta_h = jnp.sum(dl * kk, axis=-1, keepdims=True) + jnp.sum(d_rhs * v, axis=-1, keepdims=True)
        d_gap = d_kk * kk + d_qk * qk
        d_cum_h = jnp.sum(d_gap - d_gap.T, axis=-1, keepdims=True)
        d_q = dot32(d_qk, k, 1, 0) * scale
        d_k = dot32(d_qk, q, 0, 0) + dot32(d_kk + d_kk.T, k, 1, 0)
        d_v = d_rhs * beta
        d_beta = d_beta + jnp.where(lane == h, d_beta_h, 0.0)
        d_cum = d_cum + jnp.where(lane == H + h, d_cum_h, 0.0)
        d_q_raw = q_r * d_q - q_raw * (q_r * q_r * q_r) * jnp.sum(d_q * q_raw, axis=-1, keepdims=True)
        d_k_raw = k_r * d_k - k_raw * (k_r * k_r * k_r) * jnp.sum(d_k * k_raw, axis=-1, keepdims=True)
        for c, d_y in ((cq, d_q_raw * q_slope), (ck, d_k_raw * k_slope), (cv, d_v * v_slope)):
            d_pre, d_taps = conv_grad(pre_ref[:, c], d_y, taps_ref[:, c], blk.keeps)
            dpre_ref[:, c] = d_pre.astype(BF16)
            for j in range(CONV):
                dtaps_ref[j : j + 1, c] = d_taps[j]
    d_log = dot32(blk.low_f, d_cum, 0, 0)
    d_shifted = d_log * (-blk.rate) * sigmoid(blk.shifted)
    d_bd = d_beta * blk.beta * (1.0 - blk.beta) + d_shifted
    dpre_ref[:, QKV + VD :] = d_bd.astype(BF16)
    dgain_ref[...] = d_gain
    ddec_ref[0:1] = jnp.sum(d_log * blk.logdecay, axis=0, keepdims=True)
    ddec_ref[1:2] = jnp.sum(d_shifted, axis=0, keepdims=True)


def vmem_specs(count):
    return [pl.BlockSpec(memory_space=pltpu.VMEM)] * count


def smem_specs(count):
    return [pl.BlockSpec(memory_space=pltpu.SMEM)] * count


def mixer_fwd(lengths, offsets, pre, taps, gain, dec):
    n = pre.shape[0]
    return pl.pallas_call(
        mixer_fwd_kernel,
        out_shape=(
            jax.ShapeDtypeStruct((n, VD), BF16),
            jax.ShapeDtypeStruct((n, H * n), F32),
            jax.ShapeDtypeStruct((n, VD), F32),
            jax.ShapeDtypeStruct((n, VD), F32),
        ),
        in_specs=smem_specs(2) + vmem_specs(4),
        out_specs=vmem_specs(4),
        name="mixer_fwd",
    )(lengths, offsets, pre, taps, gain, dec)


def mixer_bwd(lengths, offsets, pre, taps, gain, dec, inv, upd, out, d_mixed):
    n = pre.shape[0]
    return pl.pallas_call(
        mixer_bwd_kernel,
        out_shape=(
            jax.ShapeDtypeStruct((n, QKV + VD + SMALL), BF16),
            jax.ShapeDtypeStruct((CONV, QKV), F32),
            jax.ShapeDtypeStruct((1, DV), F32),
            jax.ShapeDtypeStruct((2, SMALL), F32),
        ),
        in_specs=smem_specs(2) + vmem_specs(8),
        out_specs=vmem_specs(4),
        name="mixer_bwd",
    )(lengths, offsets, pre, taps, gain, dec, inv, upd, out, d_mixed)


class Links:
    def __init__(self, n_dev, x_bits, y_bits, z_bits):
        self.n = n_dev
        self.x, self.y, self.z = x_bits, y_bits, z_bits
        self.me = lax.axis_index("fsdp")
        self.chip_bits = sorted(x_bits + y_bits + z_bits, reverse=True)

    def bit(self, p):
        return lax.shift_right_logical(self.me, p) & 1

    def swap(self, array, p):
        return lax.ppermute(array, "fsdp", [(i, i ^ (1 << p)) for i in range(self.n)])

    def halve(self, array, bits, p):
        dim = bits.index(p)
        mine = self.bit(p)
        send = lax.dynamic_index_in_dim(array, 1 - mine, dim, keepdims=False)
        keep = lax.dynamic_index_in_dim(array, mine, dim, keepdims=False)
        return keep, self.swap(send, p), [b for b in bits if b != p]

    def grad_rows(self, left, right, order):
        bits = self.chip_bits
        slots, rows = left.shape
        p = order[0]
        dim = bits.index(p)
        above, below = 2**dim, rows // 2 ** (dim + 1)
        split = left.reshape(slots, above, 2, below)
        mine = self.bit(p)
        pick = lambda b: lax.dynamic_index_in_dim(split, b, 2, keepdims=False).reshape(slots, rows // 2)
        got = self.swap(t_mm(pick(1 - mine), right).astype(BF16), p)
        total = t_mm(pick(mine), right) + got.astype(F32)
        bits = [b for b in bits if b != p]
        per_chip = rows // 2 ** len(self.chip_bits)
        for p in order[1:]:
            total = total.astype(BF16)
            total = total.reshape((2,) * len(bits) + (per_chip, right.shape[1]))
            keep, got, bits = self.halve(total, bits, p)
            total = keep.astype(F32) + got.astype(F32)
        return total.reshape(per_chip, right.shape[1])

    def small_sum(self, array):
        bits = self.chip_bits + [0]
        width = array.shape[1]
        array = array.reshape((2,) * len(bits) + (width // 128, 128))
        for p in [0] + self.x + self.y + self.z:
            keep, got, bits = self.halve(array, bits, p)
            array = keep + got
        return array.reshape(width)


def on_device(
    tokens, cotangent, lengths, offsets, norm_mix, w_query, w_key, w_value, w_gate, w_betadecay,
    conv_weight, out_gain, w_out, norm_ffn, w_ffgate, w_ffup, w_ffdown, decay_params, *, bits,
):
    slots, width = tokens.shape
    rows = w_query.shape[0]
    n_dev = width // rows
    ff = w_ffgate.shape[1]
    link = Links(n_dev, *bits)
    core = link.bit(0)
    first_core = core == 0

    def gather(array):
        return lax.all_gather(array, "fsdp", axis=0, tiled=True)

    gain_col = jnp.concatenate([out_gain, jnp.zeros((rows - out_gain.shape[0],), BF16)])
    small_cols = jnp.concatenate(
        [w_betadecay, norm_mix[:, None], norm_ffn[:, None], conv_weight.reshape(rows, 2 * CONV), gain_col[:, None]],
        axis=1,
    )
    small_cols = jnp.pad(small_cols, ((0, 0), (0, SMALL - small_cols.shape[1])))
    full_mix = gather(jnp.concatenate([w_query, w_key, w_value, w_gate, small_cols, w_out], axis=1))
    full_ffn = gather(jnp.concatenate([w_ffgate, w_ffup], axis=1))
    full_down = gather(w_ffdown)
    proj = QKV + VD + SMALL
    small = full_mix[:, QKV + VD : proj].astype(F32)
    full_norm_mix = small[:, 2 * H]
    full_norm_ffn = small[:, 2 * H + 1]
    taps = small[:, 2 * H + 2 : 4 * H + 2].reshape(QKV, CONV).T
    gain = small[:, 4 * H + 2].reshape(n_dev, rows)[:, : out_gain.shape[0]].reshape(1, DV)
    full_in = full_mix[:, :proj]
    full_out = full_mix[:, proj:]
    dec = jnp.pad(decay_params, ((0, 0), (H, SMALL - 2 * H)))

    slot = jnp.arange(slots, dtype=jnp.int32)[:, None]
    valid = jnp.any((slot >= offsets) & (slot < offsets + lengths), axis=1)[:, None]
    top_grad = jnp.where(valid, cotangent.astype(F32), 0.0)
    top_narrow = top_grad.astype(BF16)

    tokens_wide = tokens.astype(F32)
    r_mix = lax.rsqrt(jnp.mean(tokens_wide * tokens_wide, axis=-1, keepdims=True) + 1e-05)
    mix_input = (tokens_wide * r_mix * full_norm_mix).astype(BF16)
    pre = mm(mix_input, full_in)
    mixed, inv, upd, delta_out = mixer_fwd(lengths, offsets, pre, taps, gain, dec)
    residual = tokens_wide + mm(mixed, full_out)
    r_ffn = lax.rsqrt(jnp.mean(residual * residual, axis=-1, keepdims=True) + 1e-05)
    ffn_input = (residual * r_ffn * full_norm_ffn).astype(BF16)
    up = mm(ffn_input, full_ffn)
    up_gate, up_lin = up[:, :ff], up[:, ff:]
    sig = jax.nn.sigmoid(up_gate)
    silu = up_gate * sig
    act = (silu * up_lin).astype(BF16)
    final = residual + mm(act, full_down)
    output = jnp.where(valid, final, 0.0).astype(BF16)

    half = width // 2
    top_cols = top_narrow.reshape(slots, 2, half)
    top_mine = lax.dynamic_index_in_dim(top_cols, core, 1, keepdims=False)
    top_other = link.swap(lax.dynamic_index_in_dim(top_cols, 1 - core, 1, keepdims=False), 0)
    top_both = jnp.concatenate([top_mine, top_other], axis=0)
    act_both = jnp.concatenate([act, link.swap(act, 0)], axis=0)
    order_a = link.x + link.y + link.z
    order_b = link.y + link.x + link.z
    down_a = link.grad_rows(act_both, top_both[:, : half // 2], order_a)
    down_b = link.grad_rows(act_both, top_both[:, half // 2 :], order_b)

    d_act = mm_t(top_narrow, full_down)
    d_ffgate = (d_act * up_lin * (sig * (1.0 + up_gate * (1.0 - sig)))).astype(BF16)
    d_ffup = (d_act * silu).astype(BF16)
    d_ffin = mm_t(jnp.concatenate([d_ffgate, d_ffup], axis=1), full_ffn)
    in_both = jnp.concatenate([ffn_input, link.swap(ffn_input, 0)], axis=0)
    d_mine = jnp.where(first_core, d_ffgate, d_ffup)
    d_other = link.swap(jnp.where(first_core, d_ffup, d_ffgate), 0)
    d_both = jnp.concatenate([d_mine, d_other], axis=0)
    ffn_a = link.grad_rows(in_both, d_both[:, : ff // 2], order_a)
    ffn_b = link.grad_rows(in_both, d_both[:, ff // 2 :], order_b)

    def back_norm(values, r, gain_row, d_normed):
        d_hat = d_normed * gain_row
        d_gain = jnp.sum(d_normed * values * r, axis=0)
        mean = jnp.mean(d_hat * values, axis=-1, keepdims=True)
        return r * d_hat - values * (r * r * r) * mean, d_gain

    d_res_norm, grad_norm_ffn = back_norm(residual, r_ffn, full_norm_ffn, d_ffin)
    d_residual = top_grad + d_res_norm
    d_res_narrow = d_residual.astype(BF16)
    d_mixed = mm_t(d_res_narrow, full_out)
    d_pre, d_taps, d_gain, d_dec = mixer_bwd(
        lengths, offsets, pre, taps, gain, dec, inv, upd, delta_out, d_mixed
    )
    d_min = mm_t(d_pre, full_in)
    d_tok, grad_norm_mix = back_norm(tokens_wide, r_mix, full_norm_mix, d_min)
    input_grad = d_residual + d_tok

    mix_both = jnp.concatenate([mix_input, link.swap(mix_input, 0)], axis=0)
    d_qk, d_v, d_gate = d_pre[:, : 2 * KD], d_pre[:, 2 * KD : QKV], d_pre[:, QKV : QKV + VD]
    one_mine = jnp.where(first_core, d_qk, d_gate)
    one_both = jnp.concatenate([one_mine, link.swap(jnp.where(first_core, d_gate, d_qk), 0)], axis=0)
    two_mine = jnp.where(first_core, d_v, d_res_narrow)
    two_both = jnp.concatenate([two_mine, link.swap(jnp.where(first_core, d_res_narrow, d_v), 0)], axis=0)
    left_mine = jnp.where(first_core, mix_input, mixed)
    left_both = jnp.concatenate([left_mine, link.swap(jnp.where(first_core, mixed, mix_input), 0)], axis=0)
    mix_a = link.grad_rows(mix_both, one_both, order_a)
    mix_b = link.grad_rows(left_both, two_both, order_b)

    grad_bd = t_mm(mix_input, d_pre[:, QKV + VD :])[:, : 2 * H]
    d_dec_flat = d_dec[:, H : 2 * H].reshape(1, 2 * H)
    parts = [
        grad_bd.reshape(n_dev, -1),
        grad_norm_mix.reshape(n_dev, -1),
        grad_norm_ffn.reshape(n_dev, -1),
        d_taps.T.reshape(n_dev, -1),
        d_gain.reshape(n_dev, -1),
        jnp.broadcast_to(d_dec_flat, (n_dev, 2 * H)),
    ]
    packed = jnp.concatenate(parts, axis=1)
    pad = -packed.shape[1] % 1024
    summed = link.small_sum(jnp.pad(packed, ((0, 0), (0, pad))))
    pieces = []
    first = 0
    for part in parts:
        pieces.append(summed[first : first + part.shape[1]])
        first += part.shape[1]
    bd_rows, gain_mix, gain_ffn, conv_rows, gain_rows, dec_rows = pieces

    def settle(total):
        per = total.reshape(2, total.shape[0] // 2, total.shape[1])
        mine = lax.dynamic_index_in_dim(per, core, 0, keepdims=False)
        other = link.swap(lax.dynamic_index_in_dim(per, 1 - core, 0, keepdims=False), 0)
        return jnp.where(first_core, mine, other), jnp.where(first_core, other, mine)

    down_a0, down_a1 = settle(down_a)
    down_b0, down_b1 = settle(down_b)
    grad_ffdown = jnp.concatenate([down_a0, down_b0, down_a1, down_b1], axis=1)
    gate_a, up_a = settle(ffn_a)
    gate_b, up_b = settle(ffn_b)
    grad_ffgate = jnp.concatenate([gate_a, gate_b], axis=1)
    grad_ffup = jnp.concatenate([up_a, up_b], axis=1)
    grad_qk, grad_gate = settle(mix_a)
    grad_value, grad_out = settle(mix_b)
    return (
        output,
        input_grad,
        gain_mix,
        grad_qk[:, :KD],
        grad_qk[:, KD:],
        grad_value,
        grad_gate,
        bd_rows.reshape(w_betadecay.shape),
        conv_rows.reshape(conv_weight.shape),
        gain_rows,
        grad_out,
        gain_ffn,
        grad_ffgate,
        grad_ffup,
        grad_ffdown,
        dec_rows.reshape(2, H),
    )


def axis_bits(mesh):
    coords = [d.coords for d in mesh.devices.flat]
    sizes = [1 + max(c[k] for c in coords) - min(c[k] for c in coords) for k in range(3)]
    spans, first = [], 1
    for size in sizes:
        count = size.bit_length() - 1
        spans.append(list(range(first, first + count)))
        first += count
    return spans


def solution(mesh):
    rows, vector = P("fsdp", None), P("fsdp")
    in_specs = (rows,) * 4 + (vector,) + (rows,) * 6 + (vector, rows, vector) + (rows,) * 3 + (P(),)
    out_specs = (rows,) * 2 + (vector,) + (rows,) * 6 + (vector, rows, vector) + (rows,) * 3 + (P(),)
    body = functools.partial(on_device, bits=axis_bits(mesh))
    return jax.shard_map(body, mesh=mesh, in_specs=in_specs, out_specs=out_specs, check_vma=False)
```

```python
import jax
import jax.numpy as jnp
from jax import lax
from jax.experimental import pallas as pl
from jax.experimental.pallas import tpu as pltpu
from jax.sharding import PartitionSpec as P


H = 4
DK = 128
DV = 256
CONV = 4
KD = H * DK
VD = H * DV
QKV = 2 * KD + VD
SMALL = 128
F32 = jnp.float32
BF16 = jnp.bfloat16


def dot32(a, b, ca, cb):
    return lax.dot_general(
        a, b, (((ca,), (cb,)), ((), ())), preferred_element_type=F32, precision=lax.Precision.HIGHEST
    )


def mm(a, b):
    return jnp.dot(a, b, preferred_element_type=F32)


def mm_t(a, b):
    return lax.dot_general(a, b, (((1,), (1,)), ((), ())), preferred_element_type=F32)


def t_mm(a, b):
    return lax.dot_general(a, b, (((0,), (0,)), ((), ())), preferred_element_type=F32)


def sigmoid(v):
    return 1.0 / (1.0 + jnp.exp(-v))


def find_start(slot, len_ref, off_ref):
    start = slot
    for s in range(len_ref.shape[1]):
        first = off_ref[0, s]
        inside = (slot >= first) & (slot < first + len_ref[0, s])
        start = jnp.where(inside, first, start)
    return start


def conv_sum(pre, taps, keeps):
    total = pre * taps[CONV - 1 : CONV]
    for s in range(1, CONV):
        total = total + jnp.where(keeps[s], pltpu.roll(pre, s, 0), 0.0) * taps[CONV - 1 - s : CONV - s]
    return total


def conv_grad(pre, d_sum, taps, keeps):
    n = pre.shape[0]
    d_pre = d_sum * taps[CONV - 1 : CONV]
    d_taps = [None] * CONV
    d_taps[CONV - 1] = jnp.sum(d_sum * pre, axis=0, keepdims=True)
    for s in range(1, CONV):
        masked = jnp.where(keeps[s], d_sum, 0.0)
        d_pre = d_pre + pltpu.roll(masked, n - s, 0) * taps[CONV - 1 - s : CONV - s]
        d_taps[CONV - 1 - s] = jnp.sum(masked * pltpu.roll(pre, s, 0), axis=0, keepdims=True)
    return d_pre, d_taps


class Block:
    def __init__(self, len_ref, off_ref, bd, rate_row, shift_row):
        n = bd.shape[0]
        row = lax.broadcasted_iota(jnp.int32, (n, n), 0)
        col = lax.broadcasted_iota(jnp.int32, (n, n), 1)
        slot_c = lax.broadcasted_iota(jnp.int32, (n, 1), 0)
        slot_r = lax.broadcasted_iota(jnp.int32, (1, n), 1)
        start_c = find_start(slot_c, len_ref, off_ref)
        start_r = find_start(slot_r, len_ref, off_ref)
        same = start_c == start_r
        self.row, self.col = row, col
        self.low = same & (row >= col)
        self.strict = same & (row > col)
        self.keeps = [None] + [slot_c - s >= start_c for s in range(1, CONV)]
        self.low_f = jnp.where(self.low, 1.0, 0.0)
        self.beta = sigmoid(bd)
        shifted = bd + shift_row
        self.shifted = shifted
        self.soft = jnp.maximum(shifted, 0.0) + jnp.log1p(jnp.exp(-jnp.abs(shifted)))
        self.rate = jnp.exp(rate_row)
        self.logdecay = -self.rate * self.soft
        self.cum = dot32(self.low_f, self.logdecay, 1, 0)
        self.cum_t = self.cum.T

    def decay(self, h):
        gap = self.cum[:, H + h : H + h + 1] - self.cum_t[H + h : H + h + 1, :]
        return jnp.where(self.low, jnp.exp(jnp.where(self.low, gap, 0.0)), 0.0)


def unit(v):
    r = lax.rsqrt(jnp.sum(v * v, axis=-1, keepdims=True) + 1e-06)
    return v * r, r


def head_cols(h):
    return (
        slice(h * DK, (h + 1) * DK),
        slice(KD + h * DK, KD + (h + 1) * DK),
        slice(2 * KD + h * DV, 2 * KD + (h + 1) * DV),
        slice(QKV + h * DV, QKV + (h + 1) * DV),
    )


def mixer_fwd_kernel(len_ref, off_ref, pre_ref, taps_ref, gain_ref, dec_ref, mixed_ref, inv_ref, upd_ref, out_ref):
    n = pre_ref.shape[0]
    bd = pre_ref[:, QKV + VD : QKV + VD + SMALL]
    blk = Block(len_ref, off_ref, bd, dec_ref[0:1], dec_ref[1:2])
    gain = gain_ref[...]
    lows, scores, rhs = [], [], []
    for h in range(H):
        cq, ck, cv, cg = head_cols(h)

        def conv_silu(cols):
            y = conv_sum(pre_ref[:, cols], taps_ref[:, cols], blk.keeps)
            return y * sigmoid(y)

        q = unit(conv_silu(cq))[0] * DK ** (-0.5)
        k = unit(conv_silu(ck))[0]
        v = conv_silu(cv)
        beta = blk.beta[:, h : h + 1]
        decay = blk.decay(h)
        lows.append(jnp.where(blk.strict, beta * decay * dot32(k, k, 1, 1), 0.0))
        scores.append(decay * dot32(q, k, 1, 1))
        rhs.append(beta * v)
    inv = []
    eye = jnp.where(blk.row == blk.col, 1.0, 0.0)
    pair = (blk.row // 2 == blk.col // 2) & (blk.row > blk.col)
    for h in range(H):
        inv.append(eye - jnp.where(pair, lows[h], 0.0))
    size = 2
    while size < n:
        part = (blk.row // (2 * size) == blk.col // (2 * size)) & (blk.row // size > blk.col // size)
        mids = [dot32(jnp.where(part, lows[h], 0.0), inv[h], 1, 0) for h in range(H)]
        inv = [inv[h] - dot32(inv[h], mids[h], 1, 0) for h in range(H)]
        size *= 2
    for h in range(H):
        _, _, _, cg = head_cols(h)
        cols = slice(h * DV, (h + 1) * DV)
        upd = dot32(inv[h], rhs[h], 1, 0)
        out = dot32(scores[h], upd, 1, 0)
        inv_ref[:, h * n : (h + 1) * n] = inv[h]
        upd_ref[:, cols] = upd
        out_ref[:, cols] = out
        r = lax.rsqrt(jnp.mean(out * out, axis=-1, keepdims=True) + 1e-05)
        gate = pre_ref[:, cg]
        mixed_ref[:, cols] = (out * r * gain * (gate * sigmoid(gate))).astype(BF16)


def mixer_bwd_kernel(
    len_ref, off_ref, pre_ref, taps_ref, gain_ref, dec_ref, inv_ref, upd_ref, out_ref, dmix_ref,
    dpre_ref, dtaps_ref, dgain_ref, ddec_ref,
):
    n = pre_ref.shape[0]
    bd = pre_ref[:, QKV + VD : QKV + VD + SMALL]
    blk = Block(len_ref, off_ref, bd, dec_ref[0:1], dec_ref[1:2])
    gain = gain_ref[...]
    lane = lax.broadcasted_iota(jnp.int32, (n, SMALL), 1)
    d_gain = jnp.zeros((1, DV), F32)
    d_beta = jnp.zeros((n, SMALL), F32)
    d_cum = jnp.zeros((n, SMALL), F32)
    for h in range(H):
        cq, ck, cv, cg = head_cols(h)
        cols = slice(h * DV, (h + 1) * DV)
        out = out_ref[:, cols]
        gate = pre_ref[:, cg]
        d_mixed = dmix_ref[:, cols]
        r = lax.rsqrt(jnp.mean(out * out, axis=-1, keepdims=True) + 1e-05)
        sg = sigmoid(gate)
        silu_g = gate * sg
        unit_out = out * r
        d_normed = d_mixed * silu_g
        dpre_ref[:, cg] = (d_mixed * unit_out * gain * (sg * (1.0 + gate * (1.0 - sg)))).astype(BF16)
        d_gain = d_gain + jnp.sum(d_normed * unit_out, axis=0, keepdims=True)
        d_hat = d_normed * gain
        d_out = r * d_hat - out * (r * r * r) * jnp.mean(d_hat * out, axis=-1, keepdims=True)

        def conv_silu(cols_in):
            y = conv_sum(pre_ref[:, cols_in], taps_ref[:, cols_in], blk.keeps)
            s = sigmoid(y)
            return y * s, s * (1.0 + y * (1.0 - s))

        q_raw, q_slope = conv_silu(cq)
        k_raw, k_slope = conv_silu(ck)
        v, v_slope = conv_silu(cv)
        q_unit, q_r = unit(q_raw)
        k, k_r = unit(k_raw)
        scale = DK ** (-0.5)
        q = q_unit * scale
        beta = blk.beta[:, h : h + 1]
        decay = blk.decay(h)
        kk = dot32(k, k, 1, 1)
        qk = dot32(q, k, 1, 1)
        inv = inv_ref[:, h * n : (h + 1) * n]
        upd = upd_ref[:, cols]
        d_score = dot32(d_out, upd, 1, 1)
        d_upd = dot32(decay * qk, d_out, 0, 0)
        d_rhs = dot32(inv, d_upd, 0, 0)
        d_low = jnp.where(blk.strict, -dot32(d_rhs, upd, 1, 1), 0.0)
        dl = d_low * decay
        d_kk = dl * beta
        d_qk = d_score * decay
        d_beta_h = jnp.sum(dl * kk, axis=-1, keepdims=True) + jnp.sum(d_rhs * v, axis=-1, keepdims=True)
        d_gap = d_kk * kk + d_qk * qk
        d_cum_h = jnp.sum(d_gap - d_gap.T, axis=-1, keepdims=True)
        d_q = dot32(d_qk, k, 1, 0) * scale
        d_k = dot32(d_qk, q, 0, 0) + dot32(d_kk + d_kk.T, k, 1, 0)
        d_v = d_rhs * beta
        d_beta = d_beta + jnp.where(lane == h, d_beta_h, 0.0)
        d_cum = d_cum + jnp.where(lane == H + h, d_cum_h, 0.0)
        d_q_raw = q_r * d_q - q_raw * (q_r * q_r * q_r) * jnp.sum(d_q * q_raw, axis=-1, keepdims=True)
        d_k_raw = k_r * d_k - k_raw * (k_r * k_r * k_r) * jnp.sum(d_k * k_raw, axis=-1, keepdims=True)
        for c, d_y in ((cq, d_q_raw * q_slope), (ck, d_k_raw * k_slope), (cv, d_v * v_slope)):
            d_pre, d_taps = conv_grad(pre_ref[:, c], d_y, taps_ref[:, c], blk.keeps)
            dpre_ref[:, c] = d_pre.astype(BF16)
            for j in range(CONV):
                dtaps_ref[j : j + 1, c] = d_taps[j]
    d_log = dot32(blk.low_f, d_cum, 0, 0)
    d_shifted = d_log * (-blk.rate) * sigmoid(blk.shifted)
    d_bd = d_beta * blk.beta * (1.0 - blk.beta) + d_shifted
    dpre_ref[:, QKV + VD :] = d_bd.astype(BF16)
    dgain_ref[...] = d_gain
    ddec_ref[0:1] = jnp.sum(d_log * blk.logdecay, axis=0, keepdims=True)
    ddec_ref[1:2] = jnp.sum(d_shifted, axis=0, keepdims=True)


def vmem_specs(count):
    return [pl.BlockSpec(memory_space=pltpu.VMEM)] * count


def smem_specs(count):
    return [pl.BlockSpec(memory_space=pltpu.SMEM)] * count


def mixer_fwd(lengths, offsets, pre, taps, gain, dec):
    n = pre.shape[0]
    return pl.pallas_call(
        mixer_fwd_kernel,
        out_shape=(
            jax.ShapeDtypeStruct((n, VD), BF16),
            jax.ShapeDtypeStruct((n, H * n), F32),
            jax.ShapeDtypeStruct((n, VD), F32),
            jax.ShapeDtypeStruct((n, VD), F32),
        ),
        in_specs=smem_specs(2) + vmem_specs(4),
        out_specs=vmem_specs(4),
        name="mixer_fwd",
    )(lengths, offsets, pre, taps, gain, dec)


def mixer_bwd(lengths, offsets, pre, taps, gain, dec, inv, upd, out, d_mixed):
    n = pre.shape[0]
    return pl.pallas_call(
        mixer_bwd_kernel,
        out_shape=(
            jax.ShapeDtypeStruct((n, QKV + VD + SMALL), BF16),
            jax.ShapeDtypeStruct((CONV, QKV), F32),
            jax.ShapeDtypeStruct((1, DV), F32),
            jax.ShapeDtypeStruct((2, SMALL), F32),
        ),
        in_specs=smem_specs(2) + vmem_specs(8),
        out_specs=vmem_specs(4),
        name="mixer_bwd",
    )(lengths, offsets, pre, taps, gain, dec, inv, upd, out, d_mixed)


class Links:
    def __init__(self, n_dev, x_bits, y_bits, z_bits):
        self.n = n_dev
        self.x, self.y, self.z = x_bits, y_bits, z_bits
        self.me = lax.axis_index("fsdp")
        self.chip_bits = sorted(x_bits + y_bits + z_bits, reverse=True)
        self.top = self.chip_bits[0]
        self.holder = self.bit(self.top) == self.bit(0)

    def bit(self, p):
        return lax.shift_right_logical(self.me, p) & 1

    def swap(self, array, p):
        return lax.ppermute(array, "fsdp", [(i, i ^ (1 << p)) for i in range(self.n)])

    def to_other_half(self, array, from_holder):
        pairs = [(i, i ^ (1 << self.top)) for i in range(self.n)]
        holds = lambda i: (i >> self.top) & 1 == i & 1
        return lax.ppermute(array, "fsdp", [(i, j) for i, j in pairs if holds(i) == from_holder])

    def in_order(self, p, mine, other, axis=0):
        low = self.bit(p) == 0
        return jnp.concatenate([jnp.where(low, mine, other), jnp.where(low, other, mine)], axis=axis)

    def spread(self, start, order):
        rows, held, shape = start
        for p in order:
            other = self.swap(rows, p)
            above = sum(1 for b in held if b > p)
            split = lambda a: a.reshape((2**above, 1, 2 ** (len(held) - above)) + shape)
            place = lax.broadcasted_iota(jnp.int32, (1, 2) + (1,) * (1 + len(shape)), 1)
            rows = jnp.where(place == self.bit(p), split(rows), split(other))
            held = held + [p]
            rows = rows.reshape((2 ** len(held),) + shape)
        return rows, held, shape

    def seed(self, rows):
        return rows[None], [], rows.shape

    def halve(self, array, bits, p):
        dim = bits.index(p)
        mine = self.bit(p)
        send = lax.dynamic_index_in_dim(array, 1 - mine, dim, keepdims=False)
        keep = lax.dynamic_index_in_dim(array, mine, dim, keepdims=False)
        return keep, self.swap(send, p), [b for b in bits if b != p]

    def first_half(self, left, right, bits, p):
        dim = bits.index(p)
        slots, rows = left.shape
        above, below = 2**dim, rows // 2 ** (dim + 1)
        split = left.T.reshape(above, 2, below, slots)
        mine = self.bit(p)
        pick = lambda b: lax.dynamic_index_in_dim(split, b, 1, keepdims=False).reshape(rows // 2, slots)
        return mm(pick(1 - mine), right).astype(BF16), pick(mine)

    def rest(self, sent, kept, right, bits, order):
        p = order[0]
        per = 2 * kept.shape[0] // 2 ** len(bits)
        got = self.swap(sent, p)
        total = got.astype(F32) + mm(kept, right)
        bits = [b for b in bits if b != p]
        for p in order[1:]:
            total = total.astype(BF16).reshape((2,) * len(bits) + (per, right.shape[1]))
            keep, got, bits = self.halve(total, bits, p)
            total = keep.astype(F32) + got.astype(F32)
        return total.reshape(per, right.shape[1])

    def grad_rows(self, left, right, bits, order):
        sent, kept = self.first_half(left, right, bits, order[0])
        return self.rest(sent, kept, right, bits, order)

    def small_sum(self, array):
        bits = self.chip_bits + [0]
        width = array.shape[1]
        array = array.reshape((2,) * len(bits) + (width // 128, 128))
        for p in [0] + self.z + self.x + self.y:
            keep, got, bits = self.halve(array, bits, p)
            array = keep + got
        return array.reshape(width)


def on_device(
    tokens, cotangent, lengths, offsets, norm_mix, w_query, w_key, w_value, w_gate, w_betadecay,
    conv_weight, out_gain, w_out, norm_ffn, w_ffgate, w_ffup, w_ffdown, decay_params, *, bits,
):
    slots, width = tokens.shape
    rows = w_query.shape[0]
    n_dev = width // rows
    ff = w_ffgate.shape[1]
    half_ff = ff // 2
    link = Links(n_dev, *bits)
    core = link.bit(0)
    first_core = core == 0
    chip_bits = link.chip_bits
    low_bits = chip_bits[1:]
    z_first = link.z[::-1]
    z_low = [p for p in z_first if p != link.top]

    choose = lambda a, b: jnp.where(first_core, a, b)

    def split_cores(array, axis):
        shape = array.shape[:axis] + (2, array.shape[axis] // 2) + array.shape[axis + 1 :]
        array = array.reshape(shape)
        pick = lambda b: lax.dynamic_index_in_dim(array, b, axis, keepdims=False)
        return pick(core), pick(1 - core)

    gain_col = jnp.concatenate([out_gain, jnp.zeros((rows - out_gain.shape[0],), BF16)])
    small_cols = jnp.concatenate(
        [w_betadecay, norm_mix[:, None], norm_ffn[:, None], conv_weight.reshape(rows, 2 * CONV), gain_col[:, None]],
        axis=1,
    )
    small_cols = jnp.pad(small_cols, ((0, 0), (0, SMALL - small_cols.shape[1])))
    full_mix = lax.all_gather(
        jnp.concatenate([w_query, w_key, w_value, w_gate, small_cols, w_out], axis=1), "fsdp", axis=0, tiled=True
    )
    gate_mine, gate_other = split_cores(w_ffgate, 1)
    up_mine, up_other = split_cores(w_ffup, 1)
    ffn_rows = link.in_order(
        0, jnp.concatenate([gate_mine, up_mine], axis=1), link.swap(jnp.concatenate([gate_other, up_other], axis=1), 0)
    )
    ffn_z, held, _ = link.spread(link.seed(ffn_rows), z_first)
    gate_z = (ffn_z[:, :, :half_ff], held, (2 * rows, half_ff))
    gate_w = link.spread(gate_z, link.x + link.y)[0].reshape(width, half_ff)
    up_z = (ffn_z[:, :, half_ff:], held, (2 * rows, half_ff))
    up_w = link.spread(up_z, link.y + link.x)[0].reshape(width, half_ff)
    down_rows = link.in_order(0, w_ffdown, link.swap(w_ffdown, 0))
    down_rows = jnp.where(link.holder, down_rows, link.to_other_half(down_rows, True))
    down_w = link.spread(link.seed(down_rows), link.x + link.y + z_low)[0].reshape(half_ff, width)

    proj = QKV + VD + SMALL
    small = full_mix[:, QKV + VD : proj].astype(F32)
    full_norm_mix = small[:, 2 * H]
    full_norm_ffn = small[:, 2 * H + 1]
    taps = small[:, 2 * H + 2 : 4 * H + 2].reshape(QKV, CONV).T
    gain = small[:, 4 * H + 2].reshape(n_dev, rows)[:, : out_gain.shape[0]].reshape(1, DV)
    full_in = full_mix[:, :proj]
    full_out = full_mix[:, proj:]
    dec = jnp.pad(decay_params, ((0, 0), (H, SMALL - 2 * H)))

    slot = jnp.arange(slots, dtype=jnp.int32)[:, None]
    valid = jnp.any((slot >= offsets) & (slot < offsets + lengths), axis=1)[:, None]
    top_grad = jnp.where(valid, cotangent.astype(F32), 0.0)
    top_narrow = top_grad.astype(BF16)
    top_both = jnp.concatenate([top_narrow, link.swap(top_narrow, 0)], axis=0)

    tokens_wide = tokens.astype(F32)
    r_mix = lax.rsqrt(jnp.mean(tokens_wide * tokens_wide, axis=-1, keepdims=True) + 1e-05)
    mix_input = (tokens_wide * r_mix * full_norm_mix).astype(BF16)
    pre = mm(mix_input, full_in)
    mixed, inv, upd, delta_out = mixer_fwd(lengths, offsets, pre, taps, gain, dec)
    residual = tokens_wide + mm(mixed, full_out)
    r_ffn = lax.rsqrt(jnp.mean(residual * residual, axis=-1, keepdims=True) + 1e-05)
    ffn_input = (residual * r_ffn * full_norm_ffn).astype(BF16)

    in_both = jnp.concatenate([ffn_input, link.swap(ffn_input, 0)], axis=0)
    up_gate = mm(in_both, gate_w)
    up_lin = mm(in_both, up_w)
    sig = jax.nn.sigmoid(up_gate)
    silu = up_gate * sig
    act = (silu * up_lin).astype(BF16)
    order_a = link.x + link.y + link.z
    order_b = link.y + link.x + link.z
    order_gate = link.y + link.z + link.x
    order_down = z_low[::-1] + link.x + link.y
    d_act = mm_t(top_both, down_w)
    d_gate = (d_act * up_lin * (sig * (1.0 + up_gate * (1.0 - sig)))).astype(BF16)
    d_up = (d_act * silu).astype(BF16)
    d_partial = mm_t(d_gate, gate_w) + mm_t(d_up, up_w)
    d_ffin = d_partial[:slots] + link.swap(d_partial[slots:], 0)
    sent_down, kept_down = link.first_half(act, top_both, low_bits, order_down[0])
    sent_gate, kept_gate = link.first_half(in_both, d_gate, chip_bits, order_gate[0])
    sent_up, kept_up = link.first_half(in_both, d_up, chip_bits, order_a[0])

    def back_norm(values, r, gain_row, d_normed):
        d_hat = d_normed * gain_row
        d_gain = jnp.sum(d_normed * values * r, axis=0)
        mean = jnp.mean(d_hat * values, axis=-1, keepdims=True)
        return r * d_hat - values * (r * r * r) * mean, d_gain

    d_res_norm, grad_norm_ffn = back_norm(residual, r_ffn, full_norm_ffn, d_ffin)
    d_residual = top_grad + d_res_norm
    d_res_narrow = d_residual.astype(BF16)

    def both(first, second):
        return jnp.concatenate([choose(first, second), link.swap(choose(second, first), 0)], axis=0)

    mix_both = jnp.concatenate([mix_input, link.swap(mix_input, 0)], axis=0)
    left_both = both(mix_input, mixed)
    d_res_narrow, sent_down, sent_gate, sent_up, act_late = lax.optimization_barrier(
        (d_res_narrow, sent_down, sent_gate, sent_up, act)
    )
    down_rows = link.rest(sent_down, kept_down, top_both, low_bits, order_down)
    grad_gate_rows = link.rest(sent_gate, kept_gate, d_gate, chip_bits, order_gate)
    grad_up_rows = link.rest(sent_up, kept_up, d_up, chip_bits, order_a)
    d_mixed = mm_t(d_res_narrow, full_out)
    d_mixed, mix_both, left_both = lax.optimization_barrier((d_mixed, mix_both, left_both))
    d_pre, d_taps, d_gain, d_dec = mixer_bwd(
        lengths, offsets, pre, taps, gain, dec, inv, upd, delta_out, d_mixed
    )

    one_both = both(d_pre[:, : 2 * KD], d_pre[:, QKV : QKV + VD])
    two_both = both(d_pre[:, 2 * KD : QKV], d_res_narrow)
    sent_a, kept_a = link.first_half(mix_both, one_both, chip_bits, order_a[0])
    sent_b, kept_b = link.first_half(left_both, two_both, chip_bits, order_b[0])
    d_pre, sent_a, sent_b = lax.optimization_barrier((d_pre, sent_a, sent_b))
    mix_a = link.rest(sent_a, kept_a, one_both, chip_bits, order_a)
    mix_b = link.rest(sent_b, kept_b, two_both, chip_bits, order_b)
    d_min = mm_t(d_pre, full_in)
    d_tok, grad_norm_mix = back_norm(tokens_wide, r_mix, full_norm_mix, d_min)
    input_grad = d_residual + d_tok
    partial = mm(act_late, down_w)
    final = residual + partial[:slots] + link.swap(partial[slots:], 0)
    output = jnp.where(valid, final, 0.0).astype(BF16)


    grad_bd = t_mm(mix_input, d_pre[:, QKV + VD :])[:, : 2 * H]
    d_dec_flat = d_dec[:, H : 2 * H].reshape(1, 2 * H)
    parts = [
        grad_bd.reshape(n_dev, -1),
        grad_norm_mix.reshape(n_dev, -1),
        grad_norm_ffn.reshape(n_dev, -1),
        d_taps.T.reshape(n_dev, -1),
        d_gain.reshape(n_dev, -1),
        jnp.broadcast_to(d_dec_flat, (n_dev, 2 * H)),
    ]
    packed = jnp.concatenate(parts, axis=1)
    pad = -packed.shape[1] % 1024
    summed = link.small_sum(jnp.pad(packed, ((0, 0), (0, pad))))
    pieces = []
    first = 0
    for part in parts:
        pieces.append(summed[first : first + part.shape[1]])
        first += part.shape[1]
    bd_rows, gain_mix, gain_ffn, conv_rows, gain_rows, dec_rows = pieces

    def settle(total):
        mine, other = split_cores(total, 0)
        other = link.swap(other, 0)
        return jnp.where(first_core, mine, other), jnp.where(first_core, other, mine)

    grad_ffgate = jnp.concatenate(settle(grad_gate_rows), axis=1)
    grad_ffup = jnp.concatenate(settle(grad_up_rows), axis=1)
    down_rows = down_rows + link.to_other_half(down_rows.astype(BF16), False).astype(F32)
    down_mine, down_other = split_cores(down_rows, 0)
    grad_ffdown = jnp.where(link.holder, down_mine, link.swap(down_other, 0))
    grad_qk, grad_gate = settle(mix_a)
    grad_value, grad_out = settle(mix_b)
    return (
        output,
        input_grad,
        gain_mix,
        grad_qk[:, :KD],
        grad_qk[:, KD:],
        grad_value,
        grad_gate,
        bd_rows.reshape(w_betadecay.shape),
        conv_rows.reshape(conv_weight.shape),
        gain_rows,
        grad_out,
        gain_ffn,
        grad_ffgate,
        grad_ffup,
        grad_ffdown,
        dec_rows.reshape(2, H),
    )


def axis_bits(mesh):
    coords = [d.coords for d in mesh.devices.flat]
    sizes = [1 + max(c[k] for c in coords) - min(c[k] for c in coords) for k in range(3)]
    spans, first = [], 1
    for size in sizes:
        count = size.bit_length() - 1
        spans.append(list(range(first, first + count)))
        first += count
    return spans


def solution(mesh):
    rows, vector = P("fsdp", None), P("fsdp")
    in_specs = (rows,) * 4 + (vector,) + (rows,) * 6 + (vector, rows, vector) + (rows,) * 3 + (P(),)
    out_specs = (rows,) * 2 + (vector,) + (rows,) * 6 + (vector, rows, vector) + (rows,) * 3 + (P(),)


    def body(*args):
        return on_device(*args, bits=axis_bits(mesh))

    return jax.shard_map(body, mesh=mesh, in_specs=in_specs, out_specs=out_specs, check_vma=False)
```

```python
import jax
import jax.numpy as jnp
from jax import lax
from jax.experimental import pallas as pl
from jax.experimental.pallas import tpu as pltpu
from jax.sharding import PartitionSpec as P


H = 4
DK = 128
DV = 256
CONV = 4
KD = H * DK
VD = H * DV
QKV = 2 * KD + VD
SMALL = 128
F32 = jnp.float32
BF16 = jnp.bfloat16


def dot32(a, b, ca, cb):
    return lax.dot_general(
        a, b, (((ca,), (cb,)), ((), ())), preferred_element_type=F32, precision=lax.Precision.HIGHEST
    )


def mm(a, b):
    return jnp.dot(a, b, preferred_element_type=F32)


def mm_t(a, b):
    return lax.dot_general(a, b, (((1,), (1,)), ((), ())), preferred_element_type=F32)


def t_mm(a, b):
    return lax.dot_general(a, b, (((0,), (0,)), ((), ())), preferred_element_type=F32)


def sigmoid(v):
    return 1.0 / (1.0 + jnp.exp(-v))


def find_start(slot, len_ref, off_ref):
    start = slot
    for s in range(len_ref.shape[1]):
        first = off_ref[0, s]
        inside = (slot >= first) & (slot < first + len_ref[0, s])
        start = jnp.where(inside, first, start)
    return start


def conv_sum(pre, taps, keeps):
    total = pre * taps[CONV - 1 : CONV]
    for s in range(1, CONV):
        total = total + jnp.where(keeps[s], pltpu.roll(pre, s, 0), 0.0) * taps[CONV - 1 - s : CONV - s]
    return total


def conv_grad(pre, d_sum, taps, keeps):
    n = pre.shape[0]
    d_pre = d_sum * taps[CONV - 1 : CONV]
    d_taps = [None] * CONV
    d_taps[CONV - 1] = jnp.sum(d_sum * pre, axis=0, keepdims=True)
    for s in range(1, CONV):
        masked = jnp.where(keeps[s], d_sum, 0.0)
        d_pre = d_pre + pltpu.roll(masked, n - s, 0) * taps[CONV - 1 - s : CONV - s]
        d_taps[CONV - 1 - s] = jnp.sum(masked * pltpu.roll(pre, s, 0), axis=0, keepdims=True)
    return d_pre, d_taps


class Block:
    def __init__(self, len_ref, off_ref, bd, rate_row, shift_row):
        n = bd.shape[0]
        row = lax.broadcasted_iota(jnp.int32, (n, n), 0)
        col = lax.broadcasted_iota(jnp.int32, (n, n), 1)
        slot_c = lax.broadcasted_iota(jnp.int32, (n, 1), 0)
        slot_r = lax.broadcasted_iota(jnp.int32, (1, n), 1)
        start_c = find_start(slot_c, len_ref, off_ref)
        start_r = find_start(slot_r, len_ref, off_ref)
        same = start_c == start_r
        self.row, self.col = row, col
        self.low = same & (row >= col)
        self.strict = same & (row > col)
        self.keeps = [None] + [slot_c - s >= start_c for s in range(1, CONV)]
        self.low_f = jnp.where(self.low, 1.0, 0.0)
        self.beta = sigmoid(bd)
        shifted = bd + shift_row
        self.shifted = shifted
        self.soft = jnp.maximum(shifted, 0.0) + jnp.log1p(jnp.exp(-jnp.abs(shifted)))
        self.rate = jnp.exp(rate_row)
        self.logdecay = -self.rate * self.soft
        self.cum = dot32(self.low_f, self.logdecay, 1, 0)
        self.cum_t = self.cum.T

    def decay(self, h):
        gap = self.cum[:, H + h : H + h + 1] - self.cum_t[H + h : H + h + 1, :]
        return jnp.where(self.low, jnp.exp(jnp.where(self.low, gap, 0.0)), 0.0)


def unit(v):
    r = lax.rsqrt(jnp.sum(v * v, axis=-1, keepdims=True) + 1e-06)
    return v * r, r


def head_cols(h):
    return (
        slice(h * DK, (h + 1) * DK),
        slice(KD + h * DK, KD + (h + 1) * DK),
        slice(2 * KD + h * DV, 2 * KD + (h + 1) * DV),
        slice(QKV + h * DV, QKV + (h + 1) * DV),
    )


def mixer_fwd_kernel(len_ref, off_ref, pre_ref, taps_ref, gain_ref, dec_ref, mixed_ref, inv_ref, upd_ref, out_ref, low_ref):
    n = pre_ref.shape[0]
    bd = pre_ref[:, QKV + VD : QKV + VD + SMALL]
    blk = Block(len_ref, off_ref, bd, dec_ref[0:1], dec_ref[1:2])
    gain = gain_ref[...]
    lows, scores, rhs = [], [], []
    for h in range(H):
        cq, ck, cv, cg = head_cols(h)

        def conv_silu(cols):
            y = conv_sum(pre_ref[:, cols], taps_ref[:, cols], blk.keeps)
            return y * sigmoid(y)

        q = unit(conv_silu(cq))[0] * DK ** (-0.5)
        k = unit(conv_silu(ck))[0]
        v = conv_silu(cv)
        beta = blk.beta[:, h : h + 1]
        decay = blk.decay(h)
        lows.append(jnp.where(blk.strict, beta * decay * dot32(k, k, 1, 1), 0.0))
        scores.append(decay * dot32(q, k, 1, 1))
        rhs.append(beta * v)
    inv = []
    eye = jnp.where(blk.row == blk.col, 1.0, 0.0)
    pair = (blk.row // 2 == blk.col // 2) & (blk.row > blk.col)
    for h in range(H):
        inv.append(eye - jnp.where(pair, lows[h], 0.0))
    for h in range(H):
        inv_ref[:, h * n : (h + 1) * n] = inv[h]
        low_ref[:, h * n : (h + 1) * n] = lows[h]

    def level(k, _):
        outer = lax.shift_right_logical(blk.row, k + 1) == lax.shift_right_logical(blk.col, k + 1)
        part = outer & (lax.shift_right_logical(blk.row, k) > lax.shift_right_logical(blk.col, k))
        cols = [slice(h * n, (h + 1) * n) for h in range(H)]
        old = [inv_ref[:, c] for c in cols]
        mids = [dot32(jnp.where(part, low_ref[:, c], 0.0), t, 1, 0) for c, t in zip(cols, old)]
        for c, t, mid in zip(cols, old, mids):
            inv_ref[:, c] = t - dot32(t, mid, 1, 0)
        return 0

    lax.fori_loop(1, n.bit_length() - 1, level, 0)
    for h in range(H):
        _, _, _, cg = head_cols(h)
        cols = slice(h * DV, (h + 1) * DV)
        upd = dot32(inv_ref[:, h * n : (h + 1) * n], rhs[h], 1, 0)
        out = dot32(scores[h], upd, 1, 0)
        upd_ref[:, cols] = upd
        out_ref[:, cols] = out
        r = lax.rsqrt(jnp.mean(out * out, axis=-1, keepdims=True) + 1e-05)
        gate = pre_ref[:, cg]
        mixed_ref[:, cols] = (out * r * gain * (gate * sigmoid(gate))).astype(BF16)


def mixer_bwd_kernel(
    len_ref, off_ref, pre_ref, taps_ref, gain_ref, dec_ref, inv_ref, upd_ref, out_ref, dmix_ref,
    dpre_ref, dtaps_ref, dgain_ref, ddec_ref,
):
    n = pre_ref.shape[0]
    bd = pre_ref[:, QKV + VD : QKV + VD + SMALL]
    blk = Block(len_ref, off_ref, bd, dec_ref[0:1], dec_ref[1:2])
    gain = gain_ref[...]
    lane = lax.broadcasted_iota(jnp.int32, (n, SMALL), 1)
    d_gain = jnp.zeros((1, DV), F32)
    d_beta = jnp.zeros((n, SMALL), F32)
    d_cum = jnp.zeros((n, SMALL), F32)
    for h in range(H):
        cq, ck, cv, cg = head_cols(h)
        cols = slice(h * DV, (h + 1) * DV)
        out = out_ref[:, cols]
        gate = pre_ref[:, cg]
        d_mixed = dmix_ref[:, cols]
        r = lax.rsqrt(jnp.mean(out * out, axis=-1, keepdims=True) + 1e-05)
        sg = sigmoid(gate)
        silu_g = gate * sg
        unit_out = out * r
        d_normed = d_mixed * silu_g
        dpre_ref[:, cg] = (d_mixed * unit_out * gain * (sg * (1.0 + gate * (1.0 - sg)))).astype(BF16)
        d_gain = d_gain + jnp.sum(d_normed * unit_out, axis=0, keepdims=True)
        d_hat = d_normed * gain
        d_out = r * d_hat - out * (r * r * r) * jnp.mean(d_hat * out, axis=-1, keepdims=True)

        def conv_silu(cols_in):
            y = conv_sum(pre_ref[:, cols_in], taps_ref[:, cols_in], blk.keeps)
            s = sigmoid(y)
            return y * s, s * (1.0 + y * (1.0 - s))

        q_raw, q_slope = conv_silu(cq)
        k_raw, k_slope = conv_silu(ck)
        v, v_slope = conv_silu(cv)
        q_unit, q_r = unit(q_raw)
        k, k_r = unit(k_raw)
        scale = DK ** (-0.5)
        q = q_unit * scale
        beta = blk.beta[:, h : h + 1]
        decay = blk.decay(h)
        kk = dot32(k, k, 1, 1)
        qk = dot32(q, k, 1, 1)
        inv = inv_ref[:, h * n : (h + 1) * n]
        upd = upd_ref[:, cols]
        d_score = dot32(d_out, upd, 1, 1)
        d_upd = dot32(decay * qk, d_out, 0, 0)
        d_rhs = dot32(inv, d_upd, 0, 0)
        d_low = jnp.where(blk.strict, -dot32(d_rhs, upd, 1, 1), 0.0)
        dl = d_low * decay
        d_kk = dl * beta
        d_qk = d_score * decay
        d_beta_h = jnp.sum(dl * kk, axis=-1, keepdims=True) + jnp.sum(d_rhs * v, axis=-1, keepdims=True)
        d_gap = d_kk * kk + d_qk * qk
        d_cum_h = jnp.sum(d_gap - d_gap.T, axis=-1, keepdims=True)
        d_q = dot32(d_qk, k, 1, 0) * scale
        d_k = dot32(d_qk, q, 0, 0) + dot32(d_kk + d_kk.T, k, 1, 0)
        d_v = d_rhs * beta
        d_beta = d_beta + jnp.where(lane == h, d_beta_h, 0.0)
        d_cum = d_cum + jnp.where(lane == H + h, d_cum_h, 0.0)
        d_q_raw = q_r * d_q - q_raw * (q_r * q_r * q_r) * jnp.sum(d_q * q_raw, axis=-1, keepdims=True)
        d_k_raw = k_r * d_k - k_raw * (k_r * k_r * k_r) * jnp.sum(d_k * k_raw, axis=-1, keepdims=True)
        for c, d_y in ((cq, d_q_raw * q_slope), (ck, d_k_raw * k_slope), (cv, d_v * v_slope)):
            d_pre, d_taps = conv_grad(pre_ref[:, c], d_y, taps_ref[:, c], blk.keeps)
            dpre_ref[:, c] = d_pre.astype(BF16)
            for j in range(CONV):
                dtaps_ref[j : j + 1, c] = d_taps[j]
    d_log = dot32(blk.low_f, d_cum, 0, 0)
    d_shifted = d_log * (-blk.rate) * sigmoid(blk.shifted)
    d_bd = d_beta * blk.beta * (1.0 - blk.beta) + d_shifted
    dpre_ref[:, QKV + VD :] = d_bd.astype(BF16)
    dgain_ref[...] = d_gain
    ddec_ref[0:1] = jnp.sum(d_log * blk.logdecay, axis=0, keepdims=True)
    ddec_ref[1:2] = jnp.sum(d_shifted, axis=0, keepdims=True)


def vmem_specs(count):
    return [pl.BlockSpec(memory_space=pltpu.VMEM)] * count


def smem_specs(count):
    return [pl.BlockSpec(memory_space=pltpu.SMEM)] * count


def mixer_fwd(lengths, offsets, pre, taps, gain, dec):
    n = pre.shape[0]
    return pl.pallas_call(
        mixer_fwd_kernel,
        out_shape=(
            jax.ShapeDtypeStruct((n, VD), BF16),
            jax.ShapeDtypeStruct((n, H * n), F32),
            jax.ShapeDtypeStruct((n, VD), F32),
            jax.ShapeDtypeStruct((n, VD), F32),
        ),
        in_specs=smem_specs(2) + vmem_specs(4),
        out_specs=vmem_specs(4),
        scratch_shapes=[pltpu.VMEM((n, H * n), F32)],
        name="mixer_fwd",
    )(lengths, offsets, pre, taps, gain, dec)


def mixer_bwd(lengths, offsets, pre, taps, gain, dec, inv, upd, out, d_mixed):
    n = pre.shape[0]
    return pl.pallas_call(
        mixer_bwd_kernel,
        out_shape=(
            jax.ShapeDtypeStruct((n, QKV + VD + SMALL), BF16),
            jax.ShapeDtypeStruct((CONV, QKV), F32),
            jax.ShapeDtypeStruct((1, DV), F32),
            jax.ShapeDtypeStruct((2, SMALL), F32),
        ),
        in_specs=smem_specs(2) + vmem_specs(8),
        out_specs=vmem_specs(4),
        name="mixer_bwd",
    )(lengths, offsets, pre, taps, gain, dec, inv, upd, out, d_mixed)


class Links:
    def __init__(self, n_dev, x_bits, y_bits, z_bits):
        self.n = n_dev
        self.x, self.y, self.z = x_bits, y_bits, z_bits
        self.me = lax.axis_index("fsdp")
        self.chip_bits = sorted(x_bits + y_bits + z_bits, reverse=True)
        self.top = self.chip_bits[0]
        self.holder = self.bit(self.top) == self.bit(0)

    def bit(self, p):
        return lax.shift_right_logical(self.me, p) & 1

    def swap(self, array, p):
        return lax.ppermute(array, "fsdp", [(i, i ^ (1 << p)) for i in range(self.n)])

    def to_other_half(self, array, from_holder):
        pairs = [(i, i ^ (1 << self.top)) for i in range(self.n)]
        holds = lambda i: (i >> self.top) & 1 == i & 1
        return lax.ppermute(array, "fsdp", [(i, j) for i, j in pairs if holds(i) == from_holder])

    def in_order(self, p, mine, other, axis=0):
        low = self.bit(p) == 0
        return jnp.concatenate([jnp.where(low, mine, other), jnp.where(low, other, mine)], axis=axis)

    def spread(self, start, order):
        rows, held, shape = start
        for p in order:
            other = self.swap(rows, p)
            above = sum(1 for b in held if b > p)
            split = lambda a: a.reshape((2**above, 1, 2 ** (len(held) - above)) + shape)
            place = lax.broadcasted_iota(jnp.int32, (1, 2) + (1,) * (1 + len(shape)), 1)
            rows = jnp.where(place == self.bit(p), split(rows), split(other))
            held = held + [p]
            rows = rows.reshape((2 ** len(held),) + shape)
        return rows, held, shape

    def seed(self, rows):
        return rows[None], [], rows.shape

    def halve(self, array, bits, p):
        dim = bits.index(p)
        mine = self.bit(p)
        send = lax.dynamic_index_in_dim(array, 1 - mine, dim, keepdims=False)
        keep = lax.dynamic_index_in_dim(array, mine, dim, keepdims=False)
        return keep, self.swap(send, p), [b for b in bits if b != p]

    def first_half(self, left, right, bits, p):
        dim = bits.index(p)
        slots, rows = left.shape
        above, below = 2**dim, rows // 2 ** (dim + 1)
        split = left.T.reshape(above, 2, below, slots)
        mine = self.bit(p)
        pick = lambda b: lax.dynamic_index_in_dim(split, b, 1, keepdims=False).reshape(rows // 2, slots)
        return mm(pick(1 - mine), right).astype(BF16), pick(mine)

    def rest(self, sent, kept, right, bits, order):
        p = order[0]
        per = 2 * kept.shape[0] // 2 ** len(bits)
        got = self.swap(sent, p)
        total = got.astype(F32) + mm(kept, right)
        bits = [b for b in bits if b != p]
        for p in order[1:]:
            total = total.astype(BF16).reshape((2,) * len(bits) + (per, right.shape[1]))
            keep, got, bits = self.halve(total, bits, p)
            total = keep.astype(F32) + got.astype(F32)
        return total.reshape(per, right.shape[1])

    def grad_rows(self, left, right, bits, order):
        sent, kept = self.first_half(left, right, bits, order[0])
        return self.rest(sent, kept, right, bits, order)

    def small_sum(self, array):
        bits = self.chip_bits + [0]
        width = array.shape[1]
        array = array.reshape((2,) * len(bits) + (width // 128, 128))
        for p in [0] + self.z + self.x + self.y:
            keep, got, bits = self.halve(array, bits, p)
            array = keep + got
        return array.reshape(width)


def on_device(
    tokens, cotangent, lengths, offsets, norm_mix, w_query, w_key, w_value, w_gate, w_betadecay,
    conv_weight, out_gain, w_out, norm_ffn, w_ffgate, w_ffup, w_ffdown, decay_params, *, bits,
):
    slots, width = tokens.shape
    rows = w_query.shape[0]
    n_dev = width // rows
    ff = w_ffgate.shape[1]
    half_ff = ff // 2
    link = Links(n_dev, *bits)
    core = link.bit(0)
    first_core = core == 0
    chip_bits = link.chip_bits
    low_bits = chip_bits[1:]
    z_first = link.z[::-1]
    z_low = [p for p in z_first if p != link.top]

    choose = lambda a, b: jnp.where(first_core, a, b)

    def split_cores(array, axis):
        shape = array.shape[:axis] + (2, array.shape[axis] // 2) + array.shape[axis + 1 :]
        array = array.reshape(shape)
        pick = lambda b: lax.dynamic_index_in_dim(array, b, axis, keepdims=False)
        return pick(core), pick(1 - core)

    gain_col = jnp.concatenate([out_gain, jnp.zeros((rows - out_gain.shape[0],), BF16)])
    small_cols = jnp.concatenate(
        [w_betadecay, norm_mix[:, None], norm_ffn[:, None], conv_weight.reshape(rows, 2 * CONV), gain_col[:, None]],
        axis=1,
    )
    small_cols = jnp.pad(small_cols, ((0, 0), (0, SMALL - small_cols.shape[1])))
    full_mix = lax.all_gather(
        jnp.concatenate([w_query, w_key, w_value, w_gate, small_cols, w_out], axis=1), "fsdp", axis=0, tiled=True
    )
    gate_mine, gate_other = split_cores(w_ffgate, 1)
    up_mine, up_other = split_cores(w_ffup, 1)
    ffn_rows = link.in_order(
        0, jnp.concatenate([gate_mine, up_mine], axis=1), link.swap(jnp.concatenate([gate_other, up_other], axis=1), 0)
    )
    ffn_z, held, _ = link.spread(link.seed(ffn_rows), z_first)
    gate_z = (ffn_z[:, :, :half_ff], held, (2 * rows, half_ff))
    gate_w = link.spread(gate_z, link.x + link.y)[0].reshape(width, half_ff)
    up_z = (ffn_z[:, :, half_ff:], held, (2 * rows, half_ff))
    up_w = link.spread(up_z, link.y + link.x)[0].reshape(width, half_ff)
    down_rows = link.in_order(0, w_ffdown, link.swap(w_ffdown, 0))
    down_rows = jnp.where(link.holder, down_rows, link.to_other_half(down_rows, True))
    down_w = link.spread(link.seed(down_rows), link.x + link.y + z_low)[0].reshape(half_ff, width)

    proj = QKV + VD + SMALL
    small = full_mix[:, QKV + VD : proj].astype(F32)
    full_norm_mix = small[:, 2 * H]
    full_norm_ffn = small[:, 2 * H + 1]
    taps = small[:, 2 * H + 2 : 4 * H + 2].reshape(QKV, CONV).T
    gain = small[:, 4 * H + 2].reshape(n_dev, rows)[:, : out_gain.shape[0]].reshape(1, DV)
    full_in = full_mix[:, :proj]
    full_out = full_mix[:, proj:]
    dec = jnp.pad(decay_params, ((0, 0), (H, SMALL - 2 * H)))

    slot = jnp.arange(slots, dtype=jnp.int32)[:, None]
    valid = jnp.any((slot >= offsets) & (slot < offsets + lengths), axis=1)[:, None]
    top_grad = jnp.where(valid, cotangent.astype(F32), 0.0)
    top_narrow = top_grad.astype(BF16)
    top_both = jnp.concatenate([top_narrow, link.swap(top_narrow, 0)], axis=0)

    tokens_wide = tokens.astype(F32)
    r_mix = lax.rsqrt(jnp.mean(tokens_wide * tokens_wide, axis=-1, keepdims=True) + 1e-05)
    mix_input = (tokens_wide * r_mix * full_norm_mix).astype(BF16)
    pre = mm(mix_input, full_in)
    mixed, inv, upd, delta_out = mixer_fwd(lengths, offsets, pre, taps, gain, dec)
    residual = tokens_wide + mm(mixed, full_out)
    r_ffn = lax.rsqrt(jnp.mean(residual * residual, axis=-1, keepdims=True) + 1e-05)
    ffn_input = (residual * r_ffn * full_norm_ffn).astype(BF16)

    in_both = jnp.concatenate([ffn_input, link.swap(ffn_input, 0)], axis=0)
    up_gate = mm(in_both, gate_w)
    up_lin = mm(in_both, up_w)
    sig = jax.nn.sigmoid(up_gate)
    silu = up_gate * sig
    act = (silu * up_lin).astype(BF16)
    order_a = link.x + link.y + link.z
    order_b = link.y + link.x + link.z
    order_gate = link.y + link.z + link.x
    order_down = z_low[::-1] + link.x + link.y
    d_act = mm_t(top_both, down_w)
    d_gate = (d_act * up_lin * (sig * (1.0 + up_gate * (1.0 - sig)))).astype(BF16)
    d_up = (d_act * silu).astype(BF16)
    sent_down, kept_down = link.first_half(act, top_both, low_bits, order_down[0])
    sent_gate, kept_gate = link.first_half(in_both, d_gate, chip_bits, order_gate[0])
    sent_up, kept_up = link.first_half(in_both, d_up, chip_bits, order_a[0])

    def back_norm(values, r, gain_row, d_normed):
        d_hat = d_normed * gain_row
        d_gain = jnp.sum(d_normed * values * r, axis=0)
        mean = jnp.mean(d_hat * values, axis=-1, keepdims=True)
        return r * d_hat - values * (r * r * r) * mean, d_gain

    d_gate_late, d_up_late, _, _, _ = lax.optimization_barrier((d_gate, d_up, sent_down, sent_gate, sent_up))
    d_partial = mm_t(d_gate_late, gate_w) + mm_t(d_up_late, up_w)
    d_ffin = d_partial[:slots] + link.swap(d_partial[slots:], 0)
    d_res_norm, grad_norm_ffn = back_norm(residual, r_ffn, full_norm_ffn, d_ffin)
    d_residual = top_grad + d_res_norm
    d_res_narrow = d_residual.astype(BF16)

    def both(first, second):
        return jnp.concatenate([choose(first, second), link.swap(choose(second, first), 0)], axis=0)

    mix_both = jnp.concatenate([mix_input, link.swap(mix_input, 0)], axis=0)
    left_both = both(mix_input, mixed)
    d_mixed = mm_t(d_res_narrow, full_out)
    d_mixed, mix_both, left_both = lax.optimization_barrier((d_mixed, mix_both, left_both))
    d_pre, d_taps, d_gain, d_dec = mixer_bwd(
        lengths, offsets, pre, taps, gain, dec, inv, upd, delta_out, d_mixed
    )

    one_both = both(d_pre[:, : 2 * KD], d_pre[:, QKV : QKV + VD])
    two_both = both(d_pre[:, 2 * KD : QKV], d_res_narrow)
    sent_a, kept_a = link.first_half(mix_both, one_both, chip_bits, order_a[0])
    sent_b, kept_b = link.first_half(left_both, two_both, chip_bits, order_b[0])
    d_pre, d_taps, kept_down, kept_gate, kept_up, act_late, _, _ = lax.optimization_barrier(
        (d_pre, d_taps, kept_down, kept_gate, kept_up, act, sent_a, sent_b)
    )
    down_rows = link.rest(sent_down, kept_down, top_both, low_bits, order_down)
    grad_gate_rows = link.rest(sent_gate, kept_gate, d_gate, chip_bits, order_gate)
    grad_up_rows = link.rest(sent_up, kept_up, d_up, chip_bits, order_a)
    mix_a = link.rest(sent_a, kept_a, one_both, chip_bits, order_a)
    mix_b = link.rest(sent_b, kept_b, two_both, chip_bits, order_b)
    d_min = mm_t(d_pre, full_in)
    d_tok, grad_norm_mix = back_norm(tokens_wide, r_mix, full_norm_mix, d_min)
    input_grad = d_residual + d_tok
    partial = mm(act_late, down_w)
    final = residual + partial[:slots] + link.swap(partial[slots:], 0)
    output = jnp.where(valid, final, 0.0).astype(BF16)


    grad_bd = t_mm(mix_input, d_pre[:, QKV + VD :])[:, : 2 * H]
    d_dec_flat = d_dec[:, H : 2 * H].reshape(1, 2 * H)
    parts = [
        grad_bd.reshape(n_dev, -1),
        grad_norm_mix.reshape(n_dev, -1),
        grad_norm_ffn.reshape(n_dev, -1),
        d_taps.T.reshape(n_dev, -1),
        d_gain.reshape(n_dev, -1),
        jnp.broadcast_to(d_dec_flat, (n_dev, 2 * H)),
    ]
    packed = jnp.concatenate(parts, axis=1)
    pad = -packed.shape[1] % 1024
    summed = link.small_sum(jnp.pad(packed, ((0, 0), (0, pad))))
    pieces = []
    first = 0
    for part in parts:
        pieces.append(summed[first : first + part.shape[1]])
        first += part.shape[1]
    bd_rows, gain_mix, gain_ffn, conv_rows, gain_rows, dec_rows = pieces

    def settle(total):
        mine, other = split_cores(total, 0)
        other = link.swap(other, 0)
        return jnp.where(first_core, mine, other), jnp.where(first_core, other, mine)

    grad_ffgate = jnp.concatenate(settle(grad_gate_rows), axis=1)
    grad_ffup = jnp.concatenate(settle(grad_up_rows), axis=1)
    down_rows = down_rows + link.to_other_half(down_rows.astype(BF16), False).astype(F32)
    down_mine, down_other = split_cores(down_rows, 0)
    grad_ffdown = jnp.where(link.holder, down_mine, link.swap(down_other, 0))
    grad_qk, grad_gate = settle(mix_a)
    grad_value, grad_out = settle(mix_b)
    return (
        output,
        input_grad,
        gain_mix,
        grad_qk[:, :KD],
        grad_qk[:, KD:],
        grad_value,
        grad_gate,
        bd_rows.reshape(w_betadecay.shape),
        conv_rows.reshape(conv_weight.shape),
        gain_rows,
        grad_out,
        gain_ffn,
        grad_ffgate,
        grad_ffup,
        grad_ffdown,
        dec_rows.reshape(2, H),
    )


def axis_bits(mesh):
    coords = [d.coords for d in mesh.devices.flat]
    sizes = [1 + max(c[k] for c in coords) - min(c[k] for c in coords) for k in range(3)]
    spans, first = [], 1
    for size in sizes:
        count = size.bit_length() - 1
        spans.append(list(range(first, first + count)))
        first += count
    return spans


def solution(mesh):
    rows, vector = P("fsdp", None), P("fsdp")
    in_specs = (rows,) * 4 + (vector,) + (rows,) * 6 + (vector, rows, vector) + (rows,) * 3 + (P(),)
    out_specs = (rows,) * 2 + (vector,) + (rows,) * 6 + (vector, rows, vector) + (rows,) * 3 + (P(),)


    def body(*args):
        return on_device(*args, bits=axis_bits(mesh))

    return jax.shard_map(body, mesh=mesh, in_specs=in_specs, out_specs=out_specs, check_vma=False)
```

```python
import jax
import jax.numpy as jnp
from jax import lax
from jax.experimental import pallas as pl
from jax.experimental.pallas import tpu as pltpu
from jax.sharding import PartitionSpec as P


H = 4
DK = 128
DV = 256
CONV = 4
KD = H * DK
VD = H * DV
QKV = 2 * KD + VD
SMALL = 128
F32 = jnp.float32
BF16 = jnp.bfloat16


def dot32(a, b, ca, cb):
    return lax.dot_general(
        a, b, (((ca,), (cb,)), ((), ())), preferred_element_type=F32, precision=lax.Precision.HIGHEST
    )


def mm(a, b):
    return jnp.dot(a, b, preferred_element_type=F32)


def mm_t(a, b):
    return lax.dot_general(a, b, (((1,), (1,)), ((), ())), preferred_element_type=F32)


def t_mm(a, b):
    return lax.dot_general(a, b, (((0,), (0,)), ((), ())), preferred_element_type=F32)


def sigmoid(v):
    return 1.0 / (1.0 + jnp.exp(-v))


def find_start(slot, len_ref, off_ref):
    start = slot
    for s in range(len_ref.shape[1]):
        first = off_ref[0, s]
        inside = (slot >= first) & (slot < first + len_ref[0, s])
        start = jnp.where(inside, first, start)
    return start


def conv_sum(pre, taps, keeps):
    total = pre * taps[CONV - 1 : CONV]
    for s in range(1, CONV):
        total = total + jnp.where(keeps[s], pltpu.roll(pre, s, 0), 0.0) * taps[CONV - 1 - s : CONV - s]
    return total


def conv_grad(pre, d_sum, taps, keeps):
    n = pre.shape[0]
    d_pre = d_sum * taps[CONV - 1 : CONV]
    d_taps = [None] * CONV
    d_taps[CONV - 1] = jnp.sum(d_sum * pre, axis=0, keepdims=True)
    for s in range(1, CONV):
        masked = jnp.where(keeps[s], d_sum, 0.0)
        d_pre = d_pre + pltpu.roll(masked, n - s, 0) * taps[CONV - 1 - s : CONV - s]
        d_taps[CONV - 1 - s] = jnp.sum(masked * pltpu.roll(pre, s, 0), axis=0, keepdims=True)
    return d_pre, d_taps


class Block:
    def __init__(self, len_ref, off_ref, bd, rate_row, shift_row):
        n = bd.shape[0]
        row = lax.broadcasted_iota(jnp.int32, (n, n), 0)
        col = lax.broadcasted_iota(jnp.int32, (n, n), 1)
        slot_c = lax.broadcasted_iota(jnp.int32, (n, 1), 0)
        slot_r = lax.broadcasted_iota(jnp.int32, (1, n), 1)
        start_c = find_start(slot_c, len_ref, off_ref)
        start_r = find_start(slot_r, len_ref, off_ref)
        same = start_c == start_r
        self.row, self.col = row, col
        self.low = same & (row >= col)
        self.strict = same & (row > col)
        self.keeps = [None] + [slot_c - s >= start_c for s in range(1, CONV)]
        self.low_f = jnp.where(self.low, 1.0, 0.0)
        self.beta = sigmoid(bd)
        shifted = bd + shift_row
        self.shifted = shifted
        self.soft = jnp.maximum(shifted, 0.0) + jnp.log1p(jnp.exp(-jnp.abs(shifted)))
        self.rate = jnp.exp(rate_row)
        self.logdecay = -self.rate * self.soft
        self.cum = dot32(self.low_f, self.logdecay, 1, 0)
        self.cum_t = self.cum.T

    def decay(self, h):
        gap = self.cum[:, H + h : H + h + 1] - self.cum_t[H + h : H + h + 1, :]
        return jnp.where(self.low, jnp.exp(jnp.where(self.low, gap, 0.0)), 0.0)


def unit(v):
    r = lax.rsqrt(jnp.sum(v * v, axis=-1, keepdims=True) + 1e-06)
    return v * r, r


def head_cols(h):
    return (
        slice(h * DK, (h + 1) * DK),
        slice(KD + h * DK, KD + (h + 1) * DK),
        slice(2 * KD + h * DV, 2 * KD + (h + 1) * DV),
        slice(QKV + h * DV, QKV + (h + 1) * DV),
    )


def mixer_fwd_kernel(len_ref, off_ref, pre_ref, taps_ref, gain_ref, dec_ref, mixed_ref, inv_ref, upd_ref, out_ref, low_ref):
    n = pre_ref.shape[0]
    bd = pre_ref[:, QKV + VD : QKV + VD + SMALL]
    blk = Block(len_ref, off_ref, bd, dec_ref[0:1], dec_ref[1:2])
    gain = gain_ref[...]
    lows, scores, rhs = [], [], []
    for h in range(H):
        cq, ck, cv, cg = head_cols(h)

        def conv_silu(cols):
            y = conv_sum(pre_ref[:, cols], taps_ref[:, cols], blk.keeps)
            return y * sigmoid(y)

        q = unit(conv_silu(cq))[0] * DK ** (-0.5)
        k = unit(conv_silu(ck))[0]
        v = conv_silu(cv)
        beta = blk.beta[:, h : h + 1]
        decay = blk.decay(h)
        lows.append(jnp.where(blk.strict, beta * decay * dot32(k, k, 1, 1), 0.0))
        scores.append(decay * dot32(q, k, 1, 1))
        rhs.append(beta * v)
    inv = []
    eye = jnp.where(blk.row == blk.col, 1.0, 0.0)
    pair = (blk.row // 2 == blk.col // 2) & (blk.row > blk.col)
    for h in range(H):
        inv.append(eye - jnp.where(pair, lows[h], 0.0))
    for h in range(H):
        inv_ref[:, h * n : (h + 1) * n] = inv[h]
        low_ref[:, h * n : (h + 1) * n] = lows[h]

    def level(k, _):
        outer = lax.shift_right_logical(blk.row, k + 1) == lax.shift_right_logical(blk.col, k + 1)
        part = outer & (lax.shift_right_logical(blk.row, k) > lax.shift_right_logical(blk.col, k))
        cols = [slice(h * n, (h + 1) * n) for h in range(H)]
        old = [inv_ref[:, c] for c in cols]
        mids = [dot32(jnp.where(part, low_ref[:, c], 0.0), t, 1, 0) for c, t in zip(cols, old)]
        for c, t, mid in zip(cols, old, mids):
            inv_ref[:, c] = t - dot32(t, mid, 1, 0)
        return 0

    lax.fori_loop(1, n.bit_length() - 1, level, 0)
    for h in range(H):
        _, _, _, cg = head_cols(h)
        cols = slice(h * DV, (h + 1) * DV)
        upd = dot32(inv_ref[:, h * n : (h + 1) * n], rhs[h], 1, 0)
        out = dot32(scores[h], upd, 1, 0)
        upd_ref[:, cols] = upd
        out_ref[:, cols] = out
        r = lax.rsqrt(jnp.mean(out * out, axis=-1, keepdims=True) + 1e-05)
        gate = pre_ref[:, cg]
        mixed_ref[:, cols] = (out * r * gain * (gate * sigmoid(gate))).astype(BF16)


def mixer_bwd_kernel(
    len_ref, off_ref, pre_ref, taps_ref, gain_ref, dec_ref, inv_ref, upd_ref, out_ref, dmix_ref,
    dpre_ref, dtaps_ref, dgain_ref, ddec_ref,
):
    n = pre_ref.shape[0]
    bd = pre_ref[:, QKV + VD : QKV + VD + SMALL]
    blk = Block(len_ref, off_ref, bd, dec_ref[0:1], dec_ref[1:2])
    gain = gain_ref[...]
    lane = lax.broadcasted_iota(jnp.int32, (n, SMALL), 1)
    d_gain = jnp.zeros((1, DV), F32)
    d_beta = jnp.zeros((n, SMALL), F32)
    d_cum = jnp.zeros((n, SMALL), F32)
    for h in range(H):
        cq, ck, cv, cg = head_cols(h)
        cols = slice(h * DV, (h + 1) * DV)
        out = out_ref[:, cols]
        gate = pre_ref[:, cg]
        d_mixed = dmix_ref[:, cols]
        r = lax.rsqrt(jnp.mean(out * out, axis=-1, keepdims=True) + 1e-05)
        sg = sigmoid(gate)
        silu_g = gate * sg
        unit_out = out * r
        d_normed = d_mixed * silu_g
        dpre_ref[:, cg] = (d_mixed * unit_out * gain * (sg * (1.0 + gate * (1.0 - sg)))).astype(BF16)
        d_gain = d_gain + jnp.sum(d_normed * unit_out, axis=0, keepdims=True)
        d_hat = d_normed * gain
        d_out = r * d_hat - out * (r * r * r) * jnp.mean(d_hat * out, axis=-1, keepdims=True)

        def conv_silu(cols_in):
            y = conv_sum(pre_ref[:, cols_in], taps_ref[:, cols_in], blk.keeps)
            s = sigmoid(y)
            return y * s, s * (1.0 + y * (1.0 - s))

        q_raw, q_slope = conv_silu(cq)
        k_raw, k_slope = conv_silu(ck)
        v, v_slope = conv_silu(cv)
        q_unit, q_r = unit(q_raw)
        k, k_r = unit(k_raw)
        scale = DK ** (-0.5)
        q = q_unit * scale
        beta = blk.beta[:, h : h + 1]
        decay = blk.decay(h)
        kk = dot32(k, k, 1, 1)
        qk = dot32(q, k, 1, 1)
        inv = inv_ref[:, h * n : (h + 1) * n]
        upd = upd_ref[:, cols]
        d_score = dot32(d_out, upd, 1, 1)
        d_upd = dot32(decay * qk, d_out, 0, 0)
        d_rhs = dot32(inv, d_upd, 0, 0)
        d_low = jnp.where(blk.strict, -dot32(d_rhs, upd, 1, 1), 0.0)
        dl = d_low * decay
        d_kk = dl * beta
        d_qk = d_score * decay
        d_beta_h = jnp.sum(dl * kk, axis=-1, keepdims=True) + jnp.sum(d_rhs * v, axis=-1, keepdims=True)
        d_gap = d_kk * kk + d_qk * qk
        d_cum_h = jnp.sum(d_gap - d_gap.T, axis=-1, keepdims=True)
        d_q = dot32(d_qk, k, 1, 0) * scale
        d_k = dot32(d_qk, q, 0, 0) + dot32(d_kk + d_kk.T, k, 1, 0)
        d_v = d_rhs * beta
        d_beta = d_beta + jnp.where(lane == h, d_beta_h, 0.0)
        d_cum = d_cum + jnp.where(lane == H + h, d_cum_h, 0.0)
        d_q_raw = q_r * d_q - q_raw * (q_r * q_r * q_r) * jnp.sum(d_q * q_raw, axis=-1, keepdims=True)
        d_k_raw = k_r * d_k - k_raw * (k_r * k_r * k_r) * jnp.sum(d_k * k_raw, axis=-1, keepdims=True)
        for c, d_y in ((cq, d_q_raw * q_slope), (ck, d_k_raw * k_slope), (cv, d_v * v_slope)):
            d_pre, d_taps = conv_grad(pre_ref[:, c], d_y, taps_ref[:, c], blk.keeps)
            dpre_ref[:, c] = d_pre.astype(BF16)
            for j in range(CONV):
                dtaps_ref[j : j + 1, c] = d_taps[j]
    d_log = dot32(blk.low_f, d_cum, 0, 0)
    d_shifted = d_log * (-blk.rate) * sigmoid(blk.shifted)
    d_bd = d_beta * blk.beta * (1.0 - blk.beta) + d_shifted
    dpre_ref[:, QKV + VD :] = d_bd.astype(BF16)
    dgain_ref[...] = d_gain
    ddec_ref[0:1] = jnp.sum(d_log * blk.logdecay, axis=0, keepdims=True)
    ddec_ref[1:2] = jnp.sum(d_shifted, axis=0, keepdims=True)


def vmem_specs(count):
    return [pl.BlockSpec(memory_space=pltpu.VMEM)] * count


def smem_specs(count):
    return [pl.BlockSpec(memory_space=pltpu.SMEM)] * count


def mixer_fwd(lengths, offsets, pre, taps, gain, dec):
    n = pre.shape[0]
    return pl.pallas_call(
        mixer_fwd_kernel,
        out_shape=(
            jax.ShapeDtypeStruct((n, VD), BF16),
            jax.ShapeDtypeStruct((n, H * n), F32),
            jax.ShapeDtypeStruct((n, VD), F32),
            jax.ShapeDtypeStruct((n, VD), F32),
        ),
        in_specs=smem_specs(2) + vmem_specs(4),
        out_specs=vmem_specs(4),
        scratch_shapes=[pltpu.VMEM((n, H * n), F32)],
        name="mixer_fwd",
    )(lengths, offsets, pre, taps, gain, dec)


def mixer_bwd(lengths, offsets, pre, taps, gain, dec, inv, upd, out, d_mixed):
    n = pre.shape[0]
    return pl.pallas_call(
        mixer_bwd_kernel,
        out_shape=(
            jax.ShapeDtypeStruct((n, QKV + VD + SMALL), BF16),
            jax.ShapeDtypeStruct((CONV, QKV), F32),
            jax.ShapeDtypeStruct((1, DV), F32),
            jax.ShapeDtypeStruct((2, SMALL), F32),
        ),
        in_specs=smem_specs(2) + vmem_specs(8),
        out_specs=vmem_specs(4),
        name="mixer_bwd",
    )(lengths, offsets, pre, taps, gain, dec, inv, upd, out, d_mixed)


class Links:
    def __init__(self, n_dev, x_bits, y_bits, z_bits):
        self.n = n_dev
        self.x, self.y, self.z = x_bits, y_bits, z_bits
        self.me = lax.axis_index("fsdp")
        self.chip_bits = sorted(x_bits + y_bits + z_bits, reverse=True)
        self.top = self.chip_bits[0]
        self.holder = self.bit(self.top) == self.bit(0)

    def bit(self, p):
        return lax.shift_right_logical(self.me, p) & 1

    def swap(self, array, p):
        return lax.ppermute(array, "fsdp", [(i, i ^ (1 << p)) for i in range(self.n)])

    def to_other_half(self, array, from_holder):
        pairs = [(i, i ^ (1 << self.top)) for i in range(self.n)]
        holds = lambda i: (i >> self.top) & 1 == i & 1
        return lax.ppermute(array, "fsdp", [(i, j) for i, j in pairs if holds(i) == from_holder])

    def in_order(self, p, mine, other, axis=0):
        low = self.bit(p) == 0
        return jnp.concatenate([jnp.where(low, mine, other), jnp.where(low, other, mine)], axis=axis)

    def spread(self, start, order):
        rows, held, shape = start
        for p in order:
            other = self.swap(rows, p)
            above = sum(1 for b in held if b > p)
            split = lambda a: a.reshape((2**above, 1, 2 ** (len(held) - above)) + shape)
            place = lax.broadcasted_iota(jnp.int32, (1, 2) + (1,) * (1 + len(shape)), 1)
            rows = jnp.where(place == self.bit(p), split(rows), split(other))
            held = held + [p]
            rows = rows.reshape((2 ** len(held),) + shape)
        return rows, held, shape

    def seed(self, rows):
        return rows[None], [], rows.shape

    def halve(self, array, bits, p):
        dim = bits.index(p)
        mine = self.bit(p)
        send = lax.dynamic_index_in_dim(array, 1 - mine, dim, keepdims=False)
        keep = lax.dynamic_index_in_dim(array, mine, dim, keepdims=False)
        return keep, self.swap(send, p), [b for b in bits if b != p]

    def first_half(self, left_t, right, bits, p):
        dim = bits.index(p)
        rows, slots = left_t.shape
        above, below = 2**dim, rows // 2 ** (dim + 1)
        split = left_t.reshape(above, 2, below, slots)
        mine = self.bit(p)
        pick = lambda b: lax.dynamic_index_in_dim(split, b, 1, keepdims=False).reshape(rows // 2, slots)
        return mm(pick(1 - mine), right).astype(BF16), pick(mine)

    def rest(self, sent, kept, right, bits, order):
        p = order[0]
        per = 2 * kept.shape[0] // 2 ** len(bits)
        got = self.swap(sent, p)
        total = got.astype(F32) + mm(kept, right)
        bits = [b for b in bits if b != p]
        for p in order[1:]:
            total = total.astype(BF16).reshape((2,) * len(bits) + (per, right.shape[1]))
            keep, got, bits = self.halve(total, bits, p)
            total = keep.astype(F32) + got.astype(F32)
        return total.reshape(per, right.shape[1])

    def grad_rows(self, left, right, bits, order):
        sent, kept = self.first_half(left, right, bits, order[0])
        return self.rest(sent, kept, right, bits, order)

    def small_sum(self, array):
        bits = self.chip_bits + [0]
        width = array.shape[1]
        array = array.reshape((2,) * len(bits) + (width // 128, 128))
        for p in [0] + self.z + self.x + self.y:
            keep, got, bits = self.halve(array, bits, p)
            array = keep + got
        return array.reshape(width)


def on_device(
    tokens, cotangent, lengths, offsets, norm_mix, w_query, w_key, w_value, w_gate, w_betadecay,
    conv_weight, out_gain, w_out, norm_ffn, w_ffgate, w_ffup, w_ffdown, decay_params, *, bits,
):
    slots, width = tokens.shape
    rows = w_query.shape[0]
    n_dev = width // rows
    ff = w_ffgate.shape[1]
    half_ff = ff // 2
    link = Links(n_dev, *bits)
    core = link.bit(0)
    first_core = core == 0
    chip_bits = link.chip_bits
    low_bits = chip_bits[1:]
    z_first = link.z[::-1]
    z_low = [p for p in z_first if p != link.top]

    choose = lambda a, b: jnp.where(first_core, a, b)

    def split_cores(array, axis):
        shape = array.shape[:axis] + (2, array.shape[axis] // 2) + array.shape[axis + 1 :]
        array = array.reshape(shape)
        pick = lambda b: lax.dynamic_index_in_dim(array, b, axis, keepdims=False)
        return pick(core), pick(1 - core)

    gain_col = jnp.concatenate([out_gain, jnp.zeros((rows - out_gain.shape[0],), BF16)])
    small_cols = jnp.concatenate(
        [w_betadecay, norm_mix[:, None], norm_ffn[:, None], conv_weight.reshape(rows, 2 * CONV), gain_col[:, None]],
        axis=1,
    )
    small_cols = jnp.pad(small_cols, ((0, 0), (0, SMALL - small_cols.shape[1])))
    full_mix = lax.all_gather(
        jnp.concatenate([w_query, w_key, w_value, w_gate, small_cols, w_out], axis=1), "fsdp", axis=0, tiled=True
    )
    gate_mine, gate_other = split_cores(w_ffgate, 1)
    up_mine, up_other = split_cores(w_ffup, 1)
    ffn_rows = link.in_order(
        0, jnp.concatenate([gate_mine, up_mine], axis=1), link.swap(jnp.concatenate([gate_other, up_other], axis=1), 0)
    )
    ffn_z, held, _ = link.spread(link.seed(ffn_rows), z_first)
    gate_z = (ffn_z[:, :, :half_ff], held, (2 * rows, half_ff))
    gate_w = link.spread(gate_z, link.x + link.y)[0].reshape(width, half_ff)
    up_z = (ffn_z[:, :, half_ff:], held, (2 * rows, half_ff))
    up_w = link.spread(up_z, link.y + link.x)[0].reshape(width, half_ff)
    down_rows = link.in_order(0, w_ffdown, link.swap(w_ffdown, 0))
    down_rows = jnp.where(link.holder, down_rows, link.to_other_half(down_rows, True))
    down_w = link.spread(link.seed(down_rows), link.x + link.y + z_low)[0].reshape(half_ff, width)

    proj = QKV + VD + SMALL
    small = full_mix[:, QKV + VD : proj].astype(F32)
    full_norm_mix = small[:, 2 * H]
    full_norm_ffn = small[:, 2 * H + 1]
    taps = small[:, 2 * H + 2 : 4 * H + 2].reshape(QKV, CONV).T
    gain = small[:, 4 * H + 2].reshape(n_dev, rows)[:, : out_gain.shape[0]].reshape(1, DV)
    full_in = full_mix[:, :proj]
    full_out = full_mix[:, proj:]
    dec = jnp.pad(decay_params, ((0, 0), (H, SMALL - 2 * H)))

    slot = jnp.arange(slots, dtype=jnp.int32)[:, None]
    valid = jnp.any((slot >= offsets) & (slot < offsets + lengths), axis=1)[:, None]
    top_grad = jnp.where(valid, cotangent.astype(F32), 0.0)
    top_narrow = top_grad.astype(BF16)
    top_both = jnp.concatenate([top_narrow, link.swap(top_narrow, 0)], axis=0)

    tokens_wide = tokens.astype(F32)
    r_mix = lax.rsqrt(jnp.mean(tokens_wide * tokens_wide, axis=-1, keepdims=True) + 1e-05)
    mix_input = (tokens_wide * r_mix * full_norm_mix).astype(BF16)
    pre = mm(mix_input, full_in)
    mixed, inv, upd, delta_out = mixer_fwd(lengths, offsets, pre, taps, gain, dec)
    residual = tokens_wide + mm(mixed, full_out)
    r_ffn = lax.rsqrt(jnp.mean(residual * residual, axis=-1, keepdims=True) + 1e-05)
    ffn_input = (residual * r_ffn * full_norm_ffn).astype(BF16)

    in_both = jnp.concatenate([ffn_input, link.swap(ffn_input, 0)], axis=0)
    up_gate = mm(in_both, gate_w)
    up_lin = mm(in_both, up_w)
    sig = jax.nn.sigmoid(up_gate)
    silu = up_gate * sig
    act = (silu * up_lin).astype(BF16)
    order_a = link.x + link.y + link.z
    order_b = link.y + link.x + link.z
    order_gate = link.y + link.z + link.x
    order_down = z_low[::-1] + link.x + link.y
    d_act = mm_t(top_both, down_w)
    d_gate = (d_act * up_lin * (sig * (1.0 + up_gate * (1.0 - sig)))).astype(BF16)
    d_up = (d_act * silu).astype(BF16)
    in_both_t, act_t = lax.optimization_barrier((in_both.T, act.T))
    sent_down, kept_down = link.first_half(act_t, top_both, low_bits, order_down[0])
    sent_gate, kept_gate = link.first_half(in_both_t, d_gate, chip_bits, order_gate[0])
    sent_up, kept_up = link.first_half(in_both_t, d_up, chip_bits, order_a[0])

    def back_norm(values, r, gain_row, d_normed):
        d_hat = d_normed * gain_row
        d_gain = jnp.sum(d_normed * values * r, axis=0)
        mean = jnp.mean(d_hat * values, axis=-1, keepdims=True)
        return r * d_hat - values * (r * r * r) * mean, d_gain

    d_gate_late, d_up_late, _, _, _ = lax.optimization_barrier((d_gate, d_up, sent_down, sent_gate, sent_up))
    d_partial = mm_t(d_gate_late, gate_w) + mm_t(d_up_late, up_w)
    d_ffin = d_partial[:slots] + link.swap(d_partial[slots:], 0)
    d_res_norm, grad_norm_ffn = back_norm(residual, r_ffn, full_norm_ffn, d_ffin)
    d_residual = top_grad + d_res_norm
    d_res_narrow = d_residual.astype(BF16)

    def both(first, second):
        return jnp.concatenate([choose(first, second), link.swap(choose(second, first), 0)], axis=0)

    mix_both = jnp.concatenate([mix_input, link.swap(mix_input, 0)], axis=0)
    left_both = both(mix_input, mixed)
    d_mixed = mm_t(d_res_narrow, full_out)
    d_mixed, mix_both_t, left_both_t = lax.optimization_barrier((d_mixed, mix_both.T, left_both.T))
    d_pre, d_taps, d_gain, d_dec = mixer_bwd(
        lengths, offsets, pre, taps, gain, dec, inv, upd, delta_out, d_mixed
    )

    one_both = both(d_pre[:, : 2 * KD], d_pre[:, QKV : QKV + VD])
    two_both = both(d_pre[:, 2 * KD : QKV], d_res_narrow)
    sent_a, kept_a = link.first_half(mix_both_t, one_both, chip_bits, order_a[0])
    sent_b, kept_b = link.first_half(left_both_t, two_both, chip_bits, order_b[0])
    d_pre, d_taps, kept_down, kept_gate, kept_up, act_late, _, _ = lax.optimization_barrier(
        (d_pre, d_taps, kept_down, kept_gate, kept_up, act, sent_a, sent_b)
    )
    down_rows = link.rest(sent_down, kept_down, top_both, low_bits, order_down)
    grad_gate_rows = link.rest(sent_gate, kept_gate, d_gate, chip_bits, order_gate)
    grad_up_rows = link.rest(sent_up, kept_up, d_up, chip_bits, order_a)
    mix_a = link.rest(sent_a, kept_a, one_both, chip_bits, order_a)
    mix_b = link.rest(sent_b, kept_b, two_both, chip_bits, order_b)
    d_min = mm_t(d_pre, full_in)
    d_tok, grad_norm_mix = back_norm(tokens_wide, r_mix, full_norm_mix, d_min)
    input_grad = d_residual + d_tok
    partial = mm(act_late, down_w)
    final = residual + partial[:slots] + link.swap(partial[slots:], 0)
    output = jnp.where(valid, final, 0.0).astype(BF16)


    grad_bd = t_mm(mix_input, d_pre[:, QKV + VD :])[:, : 2 * H]
    d_dec_flat = d_dec[:, H : 2 * H].reshape(1, 2 * H)
    parts = [
        grad_bd.reshape(n_dev, -1),
        grad_norm_mix.reshape(n_dev, -1),
        grad_norm_ffn.reshape(n_dev, -1),
        d_taps.T.reshape(n_dev, -1),
        d_gain.reshape(n_dev, -1),
        jnp.broadcast_to(d_dec_flat, (n_dev, 2 * H)),
    ]
    packed = jnp.concatenate(parts, axis=1)
    pad = -packed.shape[1] % 1024
    summed = link.small_sum(jnp.pad(packed, ((0, 0), (0, pad))))
    pieces = []
    first = 0
    for part in parts:
        pieces.append(summed[first : first + part.shape[1]])
        first += part.shape[1]
    bd_rows, gain_mix, gain_ffn, conv_rows, gain_rows, dec_rows = pieces

    def settle(total):
        mine, other = split_cores(total, 0)
        other = link.swap(other, 0)
        return jnp.where(first_core, mine, other), jnp.where(first_core, other, mine)

    grad_ffgate = jnp.concatenate(settle(grad_gate_rows), axis=1)
    grad_ffup = jnp.concatenate(settle(grad_up_rows), axis=1)
    down_rows = down_rows + link.to_other_half(down_rows.astype(BF16), False).astype(F32)
    down_mine, down_other = split_cores(down_rows, 0)
    grad_ffdown = jnp.where(link.holder, down_mine, link.swap(down_other, 0))
    grad_qk, grad_gate = settle(mix_a)
    grad_value, grad_out = settle(mix_b)
    return (
        output,
        input_grad,
        gain_mix,
        grad_qk[:, :KD],
        grad_qk[:, KD:],
        grad_value,
        grad_gate,
        bd_rows.reshape(w_betadecay.shape),
        conv_rows.reshape(conv_weight.shape),
        gain_rows,
        grad_out,
        gain_ffn,
        grad_ffgate,
        grad_ffup,
        grad_ffdown,
        dec_rows.reshape(2, H),
    )


def axis_bits(mesh):
    coords = [d.coords for d in mesh.devices.flat]
    sizes = [1 + max(c[k] for c in coords) - min(c[k] for c in coords) for k in range(3)]
    spans, first = [], 1
    for size in sizes:
        count = size.bit_length() - 1
        spans.append(list(range(first, first + count)))
        first += count
    return spans


def solution(mesh):
    rows, vector = P("fsdp", None), P("fsdp")
    in_specs = (rows,) * 4 + (vector,) + (rows,) * 6 + (vector, rows, vector) + (rows,) * 3 + (P(),)
    out_specs = (rows,) * 2 + (vector,) + (rows,) * 6 + (vector, rows, vector) + (rows,) * 3 + (P(),)


    def body(*args):
        return on_device(*args, bits=axis_bits(mesh))

    return jax.shard_map(body, mesh=mesh, in_specs=in_specs, out_specs=out_specs, check_vma=False)
```
